32 devices in a mesh: date: 8 (over z, x), az: 4 (over y, core).
Axes of the slice: x: 2, y: 2, z: 4, core: 2. Of those that a mesh axis runs over, the one named last changes fastest.
Arguments:
- slc: float32 [48, 2, 32, 1024], P('date', None, 'az'), may hold values from -12 to 12
- pairs: int32 [2, 512, 2], replicated, may hold values from 0 to 47, as said below
Outputs:
- interferogram: float32 [2, 512, 2, 8, 64], P(None, 'date', None, 'az')
- coherence: float32 [2, 512, 8, 64], P(None, 'date', 'az')
The draws below stay inside these ranges and needn't reach their ends.
Inputs may be any that keep to these rules, and one draw needn't show every extreme that they name: In each round the two dates of a pair differ; the pairs in the block of 64 rows of one device name exactly 8 distinct dates, and at most 2 distinct dates out of any one block of 6 dates, exactly 2 out of some block.
All inputs are finite; a program needn't handle non-finite values.
Results may differ from the reference program's by a relative error of at most 0.0014.
Values may be sent and summed in bfloat16 or wider, within the bound.
A program may use at most 64 MiB of HBM per device.

```python
import math
import jax
import jax.numpy as jnp
from jax import lax

RANGE = 1024
DATE_DEV = 6
PAIR_DEV = 64
CAP = 2
ROUNDS = 2
DATES = 48
PAIRS = 512
AZ = 32


def draw_slc(key, part):
    keys = jax.random.split(key, 9)
    scene_re = jax.random.truncated_normal(keys[0], -4.0, 4.0, (AZ, RANGE), jnp.float32)
    scene_im = jax.random.truncated_normal(keys[1], -4.0, 4.0, (AZ, RANGE), jnp.float32)
    amplitude = jnp.exp(jax.random.uniform(keys[2], (AZ, RANGE), jnp.float32, -0.7, 0.7))
    noise = jax.random.truncated_normal(keys[3], -4.0, 4.0, (DATES, 2, AZ, RANGE), jnp.float32)
    sigma = jnp.exp(jax.random.uniform(keys[5], (DATES, 1, 1), jnp.float32, math.log(0.3), math.log(3.0)))
    offset = jax.random.uniform(keys[6], (DATES, 1, 1), jnp.float32, -math.pi, math.pi)
    ramp_range = jax.random.uniform(keys[7], (DATES, 1, 1), jnp.float32, -0.03, 0.03)
    ramp_az = jax.random.uniform(keys[8], (DATES, 1, 1), jnp.float32, -0.1, 0.1)
    cols = jnp.arange(RANGE, dtype=jnp.float32)[None, None, :]
    lines = jnp.arange(AZ, dtype=jnp.float32)[None, :, None]
    phase = offset + ramp_range * cols + ramp_az * lines
    norm_factor = 1.0 / jnp.sqrt(1.0 + sigma * sigma)
    base_re = (scene_re[None] * amplitude[None] + sigma * noise[:, 0]) * norm_factor
    base_im = (scene_im[None] * amplitude[None] + sigma * noise[:, 1]) * norm_factor
    cosine = jnp.cos(phase)
    sine = jnp.sin(phase)
    out_re = jnp.clip(cosine * base_re - sine * base_im, -12.0, 12.0)
    out_im = jnp.clip(sine * base_re + cosine * base_im, -12.0, 12.0)
    return jnp.stack([out_re, out_im], axis=1).astype(jnp.float32)


def pair_block(block_key):
    device_count = PAIRS // PAIR_DEV
    slot_count = device_count * CAP
    used_count = slot_count // 2
    keys = jax.random.split(block_key, 6)
    favoured = jax.random.randint(keys[0], (), 0, device_count)
    shuffled = jax.random.permutation(keys[1], slot_count).astype(jnp.int32)
    slot_index = jnp.arange(slot_count, dtype=jnp.int32)
    slot_source = slot_index // CAP
    scores = jnp.where(slot_source == favoured, slot_index - slot_count, shuffled)
    chosen = jnp.argsort(scores, stable=True)[:used_count]
    source_keys = jax.random.split(keys[2], device_count)
    local_order = jax.vmap(lambda each_key: jax.random.permutation(each_key, DATE_DEV))(source_keys).astype(jnp.int32)
    slot_local = local_order[slot_source, slot_index % CAP]
    slot_date = slot_source * DATE_DEV + slot_local
    dates = slot_date[chosen]
    pair_index = jnp.arange(PAIR_DEV, dtype=jnp.int32)
    covering = pair_index < used_count // 2
    first = jnp.where(covering, 2 * pair_index, jax.random.randint(keys[3], (PAIR_DEV,), 0, used_count))
    stride = jax.random.randint(keys[4], (PAIR_DEV,), 1, used_count)
    second = jnp.where(covering, 2 * pair_index + 1, (first + stride) % used_count)
    order = jax.random.permutation(keys[5], PAIR_DEV)
    listed = jnp.stack([dates[first], dates[second]], axis=-1)
    return listed[order].astype(jnp.int32)


def draw_pairs(key, part):
    device_count = PAIRS // PAIR_DEV
    block_keys = jax.vmap(lambda index: jax.random.fold_in(key, index))(jnp.arange(ROUNDS * device_count))
    blocks = jax.vmap(pair_block)(block_keys)
    return blocks.reshape(ROUNDS, PAIRS, 2).astype(jnp.int32)


def setup_inputs(seed: int = 0) -> dict:
    key_of = jax.random.split(jax.random.key(seed), 3)
    slc = draw_slc(jax.random.fold_in(key_of[2], 71), 0)
    pairs = draw_pairs(jax.random.fold_in(key_of[2], 71), 0)
    return dict(slc=slc, pairs=pairs)


def multilook(field):
    shape = field.shape
    blocks = field.reshape(shape[:-2] + (shape[-2] // 4, 4, shape[-1] // 16, 16))
    return blocks.mean(axis=(-3, -1))

def pair_looks(first, second):
    first_re, first_im = (first[0], first[1])
    second_re, second_im = (second[0], second[1])
    prod_re = first_re * second_re + first_im * second_im
    prod_im = first_im * second_re - first_re * second_im
    power_a = first_re * first_re + first_im * first_im
    power_b = second_re * second_re + second_im * second_im
    return jnp.stack([multilook(prod_re), multilook(prod_im), multilook(power_a), multilook(power_b)], axis=0)

def coherence_from(padded):
    lines = padded.shape[-2] - 4
    columns = padded.shape[-1]
    az_sum = padded[..., 0:lines, :]
    for offset in range(1, 5):
        az_sum = az_sum + padded[..., offset:offset + lines, :]
    widths = [(0, 0)] * (az_sum.ndim - 1) + [(2, 2)]
    wide = jnp.pad(az_sum, widths)
    boxed = wide[..., 0:columns]
    for offset in range(1, 5):
        boxed = boxed + wide[..., offset:offset + columns]
    numer = jnp.sqrt(boxed[..., 0, :, :] ** 2 + boxed[..., 1, :, :] ** 2)
    return numer / jnp.sqrt(boxed[..., 2, :, :] * boxed[..., 3, :, :])

def reference(slc, pairs):
    quantized = lax.optimization_barrier(slc.astype(jnp.bfloat16))
    flat_pairs = pairs.reshape(-1, 2)

    def one_pair(pair_row):
        first = lax.dynamic_index_in_dim(quantized, pair_row[0], 0, keepdims=False).astype(jnp.float32)
        second = lax.dynamic_index_in_dim(quantized, pair_row[1], 0, keepdims=False).astype(jnp.float32)
        looks = pair_looks(first, second)
        padded = jnp.pad(looks, ((0, 0), (2, 2), (0, 0)))
        return (looks[0:2], coherence_from(padded))
    ifg_all, coh_all = lax.map(one_pair, flat_pairs)
    ifg_all = ifg_all.reshape((ROUNDS, PAIRS) + ifg_all.shape[1:])
    coh_all = coh_all.reshape((ROUNDS, PAIRS) + coh_all.shape[1:])
    return (ifg_all, coh_all)
```

```python
import jax
import jax.numpy as jnp
from jax import lax
from jax.experimental import pallas as pl
from jax.experimental.pallas import tpu as pltpu
from jax.sharding import PartitionSpec as P

CAP = 2
VMEM_LIMIT = 4 << 20


def with_halo(shard, sides, width):
    for axis, dim in sides:
        peers, length = (lax.axis_size(axis), shard.shape[dim])
        up = [(i, (i + 1) % peers) for i in range(peers - 1)]
        down = [(j, i) for i, j in up]
        last = lax.slice_in_dim(shard, length - width, length, axis=dim)
        first = lax.slice_in_dim(shard, 0, width, axis=dim)
        before = lax.ppermute(last, axis, up)
        after = lax.ppermute(first, axis, down)
        shard = jnp.concatenate([before, shard, after], axis=dim)
    return shard


def multilook(field):
    shape = field.shape
    blocks = field.reshape(shape[:-2] + (shape[-2] // 4, 4, shape[-1] // 16, 16))
    return blocks.mean(axis=(-3, -1))


def pair_looks(tiles):
    first = tiles[:, 0].astype(jnp.float32)
    second = tiles[:, 1].astype(jnp.float32)
    first_re, first_im = (first[:, 0], first[:, 1])
    second_re, second_im = (second[:, 0], second[:, 1])
    prod_re = first_re * second_re + first_im * second_im
    prod_im = first_im * second_re - first_re * second_im
    power_a = first_re * first_re + first_im * first_im
    power_b = second_re * second_re + second_im * second_im
    return jnp.stack(
        [multilook(prod_re), multilook(prod_im), multilook(power_a), multilook(power_b)], axis=1
    )


def coherence_from(padded):
    lines = padded.shape[-2] - 4
    columns = padded.shape[-1]
    az_sum = padded[..., 0:lines, :]
    for offset in range(1, 5):
        az_sum = az_sum + padded[..., offset : offset + lines, :]
    widths = [(0, 0)] * (az_sum.ndim - 1) + [(2, 2)]
    wide = jnp.pad(az_sum, widths)
    boxed = wide[..., 0:columns]
    for offset in range(1, 5):
        boxed = boxed + wide[..., offset : offset + columns]
    numer = jnp.sqrt(boxed[..., 0, :, :] ** 2 + boxed[..., 1, :, :] ** 2)
    return numer / jnp.sqrt(boxed[..., 2, :, :] * boxed[..., 3, :, :])


def per_device_general(slc, pairs):
    date_count = lax.axis_size("date")
    own_index = lax.axis_index("date")
    date_dev = slc.shape[0]
    pair_dev = pairs.shape[1] // date_count
    tile_shape = slc.shape[1:]
    quantized = lax.optimization_barrier(slc.astype(jnp.bfloat16))
    all_ids = jnp.arange(date_count * date_dev, dtype=jnp.int32)
    local_ids = own_index * date_dev + jnp.arange(date_dev, dtype=jnp.int32)
    local_pos = jnp.arange(date_dev, dtype=jnp.int32)
    slot_ids = jnp.arange(CAP, dtype=jnp.int32)
    looks_list = []
    for round_index in range(pairs.shape[0]):
        block = pairs[round_index]
        own_pairs = lax.dynamic_slice_in_dim(block, own_index * pair_dev, pair_dev, 0)
        entries = own_pairs.reshape(-1)
        wanted = block.reshape(date_count, 2 * pair_dev)
        needed = jnp.any(wanted[:, :, None] == local_ids[None, None, :], axis=1).astype(jnp.int32)
        ranks = jnp.cumsum(needed, axis=1) - needed
        picked = needed[:, None, :] * (ranks[:, None, :] == slot_ids[None, :, None]).astype(
            jnp.int32
        )
        source_local = jnp.sum(picked * local_pos[None, None, :], axis=2)
        present = jnp.sum(picked, axis=2) > 0
        outgoing = jnp.take(quantized, source_local.reshape(-1), axis=0).reshape(
            (date_count, CAP) + tile_shape
        )
        outgoing = jnp.where(present[:, :, None, None, None], outgoing, jnp.zeros((), jnp.bfloat16))
        incoming = lax.all_to_all(outgoing, "date", split_axis=0, concat_axis=0, tiled=True)
        matches = entries[:, None] == all_ids[None, :]
        my_need = jnp.any(matches, axis=0).astype(jnp.int32).reshape(date_count, date_dev)
        my_rank = (jnp.cumsum(my_need, axis=1) - my_need).reshape(-1)
        entry_slot = jnp.sum(jnp.where(matches, my_rank[None, :], 0), axis=1)
        position = entries // date_dev * CAP + entry_slot
        fetched = jnp.take(incoming.reshape((date_count * CAP,) + tile_shape), position, axis=0)
        looks = pair_looks(fetched.reshape((pair_dev, 2) + tile_shape))
        looks_list.append(looks)
    stacked = jnp.stack(looks_list, axis=0)
    padded = with_halo(stacked, (("az", 3),), 2)
    coherence = coherence_from(padded)
    interferogram = stacked[:, :, 0:2]
    return (interferogram, coherence)


LINES, SAMPLES = 4, 16
STEPS = ((0, 2, 2), (0, 2, 1), (1, 8, 8), (1, 8, 4), (1, 8, 2), (1, 8, 1))


def iota(shape, dim):
    return lax.broadcasted_iota(jnp.int32, shape, dim)


def place_of(leaf):
    bit = [(leaf >> n) & 1 for n in range(6)]
    return 32 * bit[3] + 16 * bit[4] + 8 * bit[5] + 4 * bit[0] + 2 * bit[1] + bit[2]


def rolled(x, shift, dim):
    return pltpu.roll(x, shift % x.shape[dim], dim)


def join(one, two, dim, unit, dist, phase):
    low = ((iota(one.shape, dim) - unit * phase) & (unit * dist)) == 0
    kept = jnp.where(low, one, two)
    other = jnp.where(low, two, one)
    return kept + rolled(other, -unit * dist, dim)


def cell_sums(real, imag):
    count = len(real)
    couples = [(i, j) for i in range(count) for j in range(i + 1, count)]

    def quantity(place):
        if place < len(couples):
            i, j = couples[place]
            return real[i] * real[j] + imag[i] * imag[j]
        place -= len(couples)
        if place < len(couples):
            i, j = couples[place]
            return imag[i] * real[j] - real[i] * imag[j]
        i = place - len(couples)
        return real[i] * real[i] + imag[i] * imag[i]

    def build(level, base, phases):
        if level == 0:
            return quantity(place_of(base))
        dim, unit, dist = STEPS[level - 1]
        moved = tuple(p + dist if d == dim else p for d, p in enumerate(phases))
        one = build(level - 1, base, phases)
        two = build(level - 1, base + (1 << (level - 1)), moved)
        return join(one, two, dim, unit, dist, phases[dim])

    return build(len(STEPS), 0, (0, 0))


def in_three(x):
    parts = []
    for _ in range(3):
        part = x.astype(jnp.bfloat16)
        parts.append(part)
        x = x - part.astype(jnp.float32)
    return jnp.concatenate(parts, 0)


def sample_order():
    src, dst = iota((128, 128), 0), iota((128, 128), 1)
    hit = dst == (src % SAMPLES) * (128 // SAMPLES) + src // SAMPLES
    return jnp.where(hit, 1.0 / 8, 0.0).astype(jnp.bfloat16)


def table_of(tiles):
    lane, sub = iota((8, 128), 1), iota((8, 128), 0)
    tiles = list(tiles)
    for b in range(3):
        dist = 8 << b
        low = (lane & dist) == 0
        for j in range(8):
            if not j >> b & 1:
                one, two = tiles[j], tiles[j | 1 << b]
                tiles[j] = jnp.where(low, one, rolled(two, dist, 1))
                tiles[j | 1 << b] = jnp.where(low, rolled(one, -dist, 1), two)
    even, first = (sub & 1) == 0, lane < 64
    out = []
    for tile in tiles:
        far = rolled(tile, 64, 1)
        moved = jnp.where(even, rolled(far, -1, 0), rolled(far, 1, 0))
        out.append(jnp.where(even == first, tile, moved))
    return out


def box_of(own, before, after):
    lane = iota(own.shape, 1)
    first = lane < 64
    both = own + rolled(own, 64, 1)
    both = both + jnp.where(first, before + rolled(before, 64, 1), before)
    both = both + jnp.where(first, after, after + rolled(after, 64, 1))
    cell = lane & 63
    out = both
    for o in (-2, -1, 1, 2):
        valid = (cell + o >= 0) & (cell + o < 64)
        out = out + jnp.where(valid, rolled(both, -o, 1), 0.0)
    return out


def pick(places, values):
    return jnp.where(iota((192, 128), 0) & 63 == places, values, 0.0)


def picks(rank_a, rank_b, count):
    first = iota(rank_a.shape, 1) < 64
    low, high = jnp.minimum(rank_a, rank_b), jnp.maximum(rank_a, rank_b)
    couples = count * (count - 1) // 2
    place = ((low * (2 * count - 1 - low)) >> 1) + high - low - 1
    sign = jnp.where(first | (rank_a < rank_b), 1.0, -1.0)
    products = pick(place + jnp.where(first, 0, couples), sign)
    powers = pick(2 * couples + jnp.where(first, rank_a, rank_b), jnp.ones_like(sign))
    return products, powers


MESH = pl.DeviceIdType.MESH


def list_dates(pairs, dates, peers):
    length = pairs.shape[1]
    part = length // peers
    date = iota((dates, length), 0)
    named = (pairs[0:1] == date) | (pairs[1:2] == date)
    parts = iota((length, 128), 0) // part == iota((length, 128), 1)
    dims = (((1,), (0,)), ((), ()))
    one = jnp.bfloat16
    counts = lax.dot_general(
        named.astype(jnp.float32).astype(one),
        parts.astype(jnp.float32).astype(one),
        dims,
        preferred_element_type=jnp.float32,
    )
    needed = counts > 0.5
    before = iota((dates, dates), 1) < iota((dates, dates), 0)
    rank = lax.dot_general(
        before.astype(jnp.float32).astype(one),
        needed.astype(jnp.float32).astype(one),
        dims,
        preferred_element_type=jnp.float32,
    )
    rank = jnp.where(needed, rank, -1.0).astype(jnp.int32)
    date = iota(rank.shape, 0)
    rows = [jnp.sum(jnp.where(rank == k, date, 0), axis=0, keepdims=True) for k in range(peers)]
    return jnp.concatenate(rows, 0)


def stack_kernel(
    slc_ref,
    pairs_hbm,
    table,
    boxed_ref,
    chosen,
    lines,
    sent,
    held,
    full,
    sums,
    tiles,
    halo,
    listed,
    ids,
    pairs_ref,
    pairs_sem,
    line_sem,
    send_a,
    recv_a,
    send_b,
    recv_b,
    send_h,
    recv_h,
    list_sem,
):
    peers, az_size = lax.axis_size("date"), lax.axis_size("az")
    me, az = lax.axis_index("date"), lax.axis_index("az")
    date_dev = slc_ref.shape[0]
    rounds = pairs_ref.shape[0]
    width = slc_ref.shape[3] // peers
    images_dev = 2 * date_dev
    sides = ((-1, az > 0), (1, az < az_size - 1))

    named = pltpu.make_async_copy(pairs_hbm, pairs_ref, pairs_sem)
    barrier = pltpu.get_barrier_semaphore()
    for n in range(date_dev):
        pltpu.make_async_copy(slc_ref.at[n], lines.at[n], line_sem).start()
    named.start()
    for o in range(1, peers):
        pl.semaphore_signal(
            barrier, inc=1, device_id={"date": lax.rem(me + o, peers)}, device_id_type=MESH
        )
    for step, there in sides:

        @pl.when(there)
        def _():
            pl.semaphore_signal(barrier, inc=1, device_id={"az": az + step}, device_id_type=MESH)

    rows_date = sent.shape[1] // date_dev
    pltpu.make_async_copy(slc_ref, lines, line_sem).wait()
    for n in range(date_dev):
        for j in range(peers):
            part = lines[n, :, :, j * width : (j + 1) * width]
            at = slice(n * rows_date, (n + 1) * rows_date)
            sent[j, at] = part.reshape(rows_date, width).astype(jnp.bfloat16)
    greeted = peers - 1 + (az > 0).astype(jnp.int32) + (az < az_size - 1).astype(jnp.int32)
    pl.semaphore_wait(barrier, greeted)

    def images(o):
        peer = lax.rem(me + o, peers)
        return pltpu.make_async_remote_copy(
            src_ref=sent.at[peer],
            dst_ref=held.at[me],
            send_sem=send_a,
            recv_sem=recv_a.at[o],
            device_id={"date": peer},
            device_id_type=MESH,
        )

    for o in range(1, peers):
        images(o).start()
    named.wait()
    for r in range(rounds):
        listed[r * peers : (r + 1) * peers, :] = list_dates(
            pairs_ref[r], date_dev * peers, peers
        )
    fetch = pltpu.make_async_copy(listed, ids, list_sem)
    fetch.start()
    order = sample_order()

    def take(owner, block):
        spread = jnp.dot(block, order, preferred_element_type=jnp.float32)
        for image in range(images_dev):
            for group in range(2):
                row = image * 8 + group * LINES
                at = (owner * images_dev + image, pl.ds(group, LINES, stride=2))
                full[at] = spread[row : row + LINES]

    take(me, sent[me])
    fetch.wait()
    lane = iota((1, 128), 1)
    for r in range(rounds):
        ranks = []
        for c in range(2):
            start = pl.multiple_of(me // 2 * 128, 128)
            near = pairs_ref[r, c : c + 1, pl.ds(start, 128)]
            own = jnp.where((lane < 64) == (lax.rem(me, 2) == 0), near, rolled(near, 64, 1))
            rank = jnp.zeros_like(own)
            for k in range(peers):
                rank = rank + (own > ids[r * peers + k, me]).astype(jnp.int32)
            ranks.append(rank)
        products, powers = picks(*ranks, peers)
        chosen[r, :128, :] = products.T.astype(jnp.bfloat16)
        chosen[r, 128:, :] = powers.T.astype(jnp.bfloat16)
    for o in range(1, peers):
        images(o).wait_recv()
        owner = lax.rem(me + peers - o, peers)
        take(owner, held[owner])

    def results(o):
        peer = lax.rem(me + o, peers)
        return pltpu.make_async_remote_copy(
            src_ref=sums.at[peer],
            dst_ref=tiles.at[me],
            send_sem=send_b,
            recv_sem=recv_b,
            device_id={"date": peer},
            device_id_type=MESH,
        )

    def serve(o, carry):
        peer = lax.rem(me + o, peers)
        for r in range(rounds):
            real, imag = [], []
            for k in range(peers):
                date = ids[r * peers + k, peer]
                real.append(full[2 * date])
                imag.append(full[2 * date + 1])
            sums[peer, r] = cell_sums(real, imag)

        @pl.when(o < peers)
        def _():
            results(o).start()

        return carry

    lax.fori_loop(1, peers + 1, serve, 0)
    tiles[me] = sums[me]
    others = pl.ds(0, peers - 1)

    def all_of(src, dst, send_sem, recv_sem):
        return pltpu.make_async_remote_copy(
            src_ref=src.at[others],
            dst_ref=dst.at[others],
            send_sem=send_sem,
            recv_sem=recv_sem,
            device_id={"date": lax.rem(me + 1, peers)},
            device_id_type=MESH,
        )

    all_of(sums, tiles, send_b, recv_b).wait_recv()
    for r in range(rounds):
        for k, tile in enumerate(table_of([tiles[j, r] for j in range(peers)])):
            table[r, 8 * k : 8 * k + 8, :] = tile

    def edge(n, step):
        return pltpu.make_async_remote_copy(
            src_ref=table,
            dst_ref=halo.at[n],
            send_sem=send_h.at[n],
            recv_sem=recv_h.at[n],
            device_id={"az": az + step},
            device_id_type=MESH,
        )

    for n, (step, there) in enumerate(sides):

        @pl.when(there)
        def _():
            edge(n, step).start()

        @pl.when(jnp.logical_not(there))
        def _():
            halo[1 - n] = jnp.zeros_like(halo[1 - n])

    for n, (step, there) in enumerate(sides):

        @pl.when(there)
        def _():
            edge(1 - n, step).wait_recv()

    for r in range(rounds):
        boxed_ref[r] = box_of(table[r], halo[1, r], halo[0, r])

    all_of(sent, held, send_a, recv_a.at[0]).wait_send()
    all_of(sums, tiles, send_b, recv_b).wait_send()
    for n, (step, there) in enumerate(sides):

        @pl.when(there)
        def _():
            edge(n, step).wait_send()


def pairs_kernel(table_ref, boxed_ref, chosen_ref, ifg_hbm, coh_hbm, ifg_ref, coh_ref, sems):
    rounds = table_ref.shape[0]

    def out(r, src, dst, n):
        rows = src.shape[0] // rounds
        at = pl.ds(rows * r, rows)
        return pltpu.make_async_copy(src.at[at], dst.at[at], sems.at[n, r])

    for r in range(rounds):
        means = jnp.dot(
            chosen_ref[r, :128, :], in_three(table_ref[r]), preferred_element_type=jnp.float32
        )
        for c in range(2):
            for row in range(2):
                part = means[64 * c : 64 * c + 64, 64 * row : 64 * row + 64]
                ifg_ref[pl.ds(256 * r + 2 * c + row, 64, stride=4), :] = part
        out(r, ifg_ref, ifg_hbm, 0).start()
        parts = jnp.dot(
            chosen_ref[r], in_three(boxed_ref[r]), preferred_element_type=jnp.float32
        )
        size = jnp.sqrt(parts[:64] * parts[:64] + parts[64:128] * parts[64:128])
        coherence = size / jnp.sqrt(parts[128:192] * parts[192:])
        for row in range(2):
            part = coherence[:, 64 * row : 64 * row + 64]
            coh_ref[pl.ds(128 * r + row, 64, stride=2), :] = part
        out(r, coh_ref, coh_hbm, 1).start()
    for r in range(rounds):
        out(r, ifg_ref, ifg_hbm, 0).wait()
        out(r, coh_ref, coh_hbm, 1).wait()


def per_device_few(slc, pairs):
    peers = lax.axis_size("date")
    rounds = pairs.shape[0]
    pair_dev = pairs.shape[1] // peers
    date_dev, _, lines, columns = slc.shape
    width = columns // peers
    rows = date_dev * 2 * lines
    cells = columns // SAMPLES
    vmem = pl.BlockSpec(memory_space=pltpu.VMEM)
    hbm = pl.BlockSpec(memory_space=pltpu.HBM)
    dma = pltpu.SemaphoreType.DMA
    found = pl.pallas_call(
        stack_kernel,
        out_shape=(
            jax.ShapeDtypeStruct((rounds, 64, 128), jnp.float32),
            jax.ShapeDtypeStruct((rounds, 64, 128), jnp.float32),
            jax.ShapeDtypeStruct((rounds, 256, 192), jnp.bfloat16),
        ),
        in_specs=[hbm, hbm],
        out_specs=(vmem,) * 3,
        scratch_shapes=[
            pltpu.VMEM(slc.shape, jnp.float32),
            pltpu.VMEM((peers, rows, width), jnp.bfloat16),
            pltpu.VMEM((peers, rows, width), jnp.bfloat16),
            pltpu.VMEM((peers * date_dev * 2, lines, width), jnp.float32),
            pltpu.VMEM((peers, rounds, 8, 128), jnp.float32),
            pltpu.VMEM((peers, rounds, 8, 128), jnp.float32),
            pltpu.VMEM((2, rounds, 64, 128), jnp.float32),
            pltpu.VMEM((rounds * peers, 128), jnp.int32),
            pltpu.SMEM((rounds * peers, 128), jnp.int32),
            pltpu.VMEM((rounds, 2, pairs.shape[1]), jnp.int32),
            dma,
            dma,
            dma,
            dma((peers,)),
            dma,
            dma,
            dma((2,)),
            dma((2,)),
            dma,
        ],
        compiler_params=pltpu.CompilerParams(
            collective_id=0, has_side_effects=True, vmem_limit_bytes=VMEM_LIMIT
        ),
    )(
        pltpu.with_memory_space_constraint(slc, pltpu.HBM),
        pltpu.with_memory_space_constraint(pairs.transpose(0, 2, 1), pltpu.HBM),
    )
    ifg_shape = (rounds * pair_dev * 2 * lines // LINES, cells)
    coh_shape = (rounds * pair_dev * lines // LINES, cells)
    ifg, coh = pl.pallas_call(
        pairs_kernel,
        out_shape=(
            jax.ShapeDtypeStruct(ifg_shape, jnp.float32),
            jax.ShapeDtypeStruct(coh_shape, jnp.float32),
        ),
        in_specs=[vmem] * 3,
        out_specs=(hbm, hbm),
        scratch_shapes=[
            pltpu.VMEM(ifg_shape, jnp.float32),
            pltpu.VMEM(coh_shape, jnp.float32),
            dma((2, rounds)),
        ],
        compiler_params=pltpu.CompilerParams(vmem_limit_bytes=VMEM_LIMIT),
    )(*found)
    return (
        ifg.reshape(rounds, pair_dev, 2, lines // LINES, cells),
        coh.reshape(rounds, pair_dev, lines // LINES, cells),
    )


def per_device(slc, pairs):
    peers = lax.axis_size("date")
    lines, columns = slc.shape[2:]
    pair_dev = pairs.shape[1] // peers
    few = (peers, pair_dev, lines, columns) == (8, 64, 2 * LINES, 64 * SAMPLES)
    return per_device_few(slc, pairs) if few else per_device_general(slc, pairs)


def solution(mesh):
    return jax.shard_map(
        per_device,
        mesh=mesh,
        in_specs=(P("date", None, "az", None), P()),
        out_specs=(P(None, "date", None, "az", None), P(None, "date", "az", None)),
        check_vma=False,
    )
```

```python
import jax
import jax.numpy as jnp
from jax import lax
from jax.experimental import pallas as pl
from jax.experimental.pallas import tpu as pltpu
from jax.sharding import PartitionSpec as P

CAP = 2
VMEM_LIMIT = 4 << 20


def with_halo(shard, sides, width):
    for axis, dim in sides:
        peers, length = (lax.axis_size(axis), shard.shape[dim])
        up = [(i, (i + 1) % peers) for i in range(peers - 1)]
        down = [(j, i) for i, j in up]
        last = lax.slice_in_dim(shard, length - width, length, axis=dim)
        first = lax.slice_in_dim(shard, 0, width, axis=dim)
        before = lax.ppermute(last, axis, up)
        after = lax.ppermute(first, axis, down)
        shard = jnp.concatenate([before, shard, after], axis=dim)
    return shard


def multilook(field):
    shape = field.shape
    blocks = field.reshape(shape[:-2] + (shape[-2] // 4, 4, shape[-1] // 16, 16))
    return blocks.mean(axis=(-3, -1))


def pair_looks(tiles):
    first = tiles[:, 0].astype(jnp.float32)
    second = tiles[:, 1].astype(jnp.float32)
    first_re, first_im = (first[:, 0], first[:, 1])
    second_re, second_im = (second[:, 0], second[:, 1])
    prod_re = first_re * second_re + first_im * second_im
    prod_im = first_im * second_re - first_re * second_im
    power_a = first_re * first_re + first_im * first_im
    power_b = second_re * second_re + second_im * second_im
    return jnp.stack(
        [multilook(prod_re), multilook(prod_im), multilook(power_a), multilook(power_b)], axis=1
    )


def coherence_from(padded):
    lines = padded.shape[-2] - 4
    columns = padded.shape[-1]
    az_sum = padded[..., 0:lines, :]
    for offset in range(1, 5):
        az_sum = az_sum + padded[..., offset : offset + lines, :]
    widths = [(0, 0)] * (az_sum.ndim - 1) + [(2, 2)]
    wide = jnp.pad(az_sum, widths)
    boxed = wide[..., 0:columns]
    for offset in range(1, 5):
        boxed = boxed + wide[..., offset : offset + columns]
    numer = jnp.sqrt(boxed[..., 0, :, :] ** 2 + boxed[..., 1, :, :] ** 2)
    return numer / jnp.sqrt(boxed[..., 2, :, :] * boxed[..., 3, :, :])


def per_device_general(slc, pairs):
    date_count = lax.axis_size("date")
    own_index = lax.axis_index("date")
    date_dev = slc.shape[0]
    pair_dev = pairs.shape[1] // date_count
    tile_shape = slc.shape[1:]
    quantized = lax.optimization_barrier(slc.astype(jnp.bfloat16))
    all_ids = jnp.arange(date_count * date_dev, dtype=jnp.int32)
    local_ids = own_index * date_dev + jnp.arange(date_dev, dtype=jnp.int32)
    local_pos = jnp.arange(date_dev, dtype=jnp.int32)
    slot_ids = jnp.arange(CAP, dtype=jnp.int32)
    looks_list = []
    for round_index in range(pairs.shape[0]):
        block = pairs[round_index]
        own_pairs = lax.dynamic_slice_in_dim(block, own_index * pair_dev, pair_dev, 0)
        entries = own_pairs.reshape(-1)
        wanted = block.reshape(date_count, 2 * pair_dev)
        needed = jnp.any(wanted[:, :, None] == local_ids[None, None, :], axis=1).astype(jnp.int32)
        ranks = jnp.cumsum(needed, axis=1) - needed
        picked = needed[:, None, :] * (ranks[:, None, :] == slot_ids[None, :, None]).astype(
            jnp.int32
        )
        source_local = jnp.sum(picked * local_pos[None, None, :], axis=2)
        present = jnp.sum(picked, axis=2) > 0
        outgoing = jnp.take(quantized, source_local.reshape(-1), axis=0).reshape(
            (date_count, CAP) + tile_shape
        )
        outgoing = jnp.where(present[:, :, None, None, None], outgoing, jnp.zeros((), jnp.bfloat16))
        incoming = lax.all_to_all(outgoing, "date", split_axis=0, concat_axis=0, tiled=True)
        matches = entries[:, None] == all_ids[None, :]
        my_need = jnp.any(matches, axis=0).astype(jnp.int32).reshape(date_count, date_dev)
        my_rank = (jnp.cumsum(my_need, axis=1) - my_need).reshape(-1)
        entry_slot = jnp.sum(jnp.where(matches, my_rank[None, :], 0), axis=1)
        position = entries // date_dev * CAP + entry_slot
        fetched = jnp.take(incoming.reshape((date_count * CAP,) + tile_shape), position, axis=0)
        looks = pair_looks(fetched.reshape((pair_dev, 2) + tile_shape))
        looks_list.append(looks)
    stacked = jnp.stack(looks_list, axis=0)
    padded = with_halo(stacked, (("az", 3),), 2)
    coherence = coherence_from(padded)
    interferogram = stacked[:, :, 0:2]
    return (interferogram, coherence)


LINES, SAMPLES = 4, 16
STEPS = ((0, 2, 2), (0, 2, 1), (1, 8, 8), (1, 8, 4), (1, 8, 2), (1, 8, 1))


def iota(shape, dim):
    return lax.broadcasted_iota(jnp.int32, shape, dim)


def place_of(leaf):
    bit = [(leaf >> n) & 1 for n in range(6)]
    return 32 * bit[3] + 16 * bit[4] + 8 * bit[5] + 4 * bit[0] + 2 * bit[1] + bit[2]


def rolled(x, shift, dim):
    return pltpu.roll(x, shift % x.shape[dim], dim)


def join(one, two, dim, unit, dist, phase):
    low = ((iota(one.shape, dim) - unit * phase) & (unit * dist)) == 0
    kept = jnp.where(low, one, two)
    other = jnp.where(low, two, one)
    return kept + rolled(other, -unit * dist, dim)


def cell_sums(real, imag):
    count = len(real)
    couples = [(i, j) for i in range(count) for j in range(i + 1, count)]

    def quantity(place):
        if place < len(couples):
            i, j = couples[place]
            return real[i] * real[j] + imag[i] * imag[j]
        place -= len(couples)
        if place < len(couples):
            i, j = couples[place]
            return imag[i] * real[j] - real[i] * imag[j]
        i = place - len(couples)
        return real[i] * real[i] + imag[i] * imag[i]

    def build(level, base, phases):
        if level == 0:
            return quantity(place_of(base))
        dim, unit, dist = STEPS[level - 1]
        moved = tuple(p + dist if d == dim else p for d, p in enumerate(phases))
        one = build(level - 1, base, phases)
        two = build(level - 1, base + (1 << (level - 1)), moved)
        return join(one, two, dim, unit, dist, phases[dim])

    return build(len(STEPS), 0, (0, 0))


def in_two(x):
    high = x.astype(jnp.bfloat16)
    low = (x - high.astype(jnp.float32)).astype(jnp.bfloat16)
    return jnp.concatenate([high, low], 0)


def sample_order():
    src, dst = iota((128, 128), 0), iota((128, 128), 1)
    hit = dst == (src % SAMPLES) * (128 // SAMPLES) + src // SAMPLES
    return jnp.where(hit, 1.0 / 8, 0.0).astype(jnp.bfloat16)


def table_of(tiles):
    lane, sub = iota((8, 128), 1), iota((8, 128), 0)
    tiles = list(tiles)
    for b in range(3):
        dist = 8 << b
        low = (lane & dist) == 0
        for j in range(8):
            if not j >> b & 1:
                one, two = tiles[j], tiles[j | 1 << b]
                tiles[j] = jnp.where(low, one, rolled(two, dist, 1))
                tiles[j | 1 << b] = jnp.where(low, rolled(one, -dist, 1), two)
    even, first = (sub & 1) == 0, lane < 64
    out = []
    for tile in tiles:
        far = rolled(tile, 64, 1)
        moved = jnp.where(even, rolled(far, -1, 0), rolled(far, 1, 0))
        out.append(jnp.where(even == first, tile, moved))
    return out


def both_rows(x):
    odd = (iota(x.shape, 0) & 1) == 1
    return x + jnp.where(odd, rolled(x, 1, 0), rolled(x, -1, 0))


def shares_of(x):
    odd = (iota(x.shape, 0) & 1) == 1
    both = both_rows(x)
    return x, jnp.where(odd, both, x), jnp.where(odd, x, both)


def box_of(both):
    cell = iota(both.shape, 1) & 63
    out = both
    for o in (-2, -1, 1, 2):
        valid = (cell + o >= 0) & (cell + o < 64)
        out = out + jnp.where(valid, rolled(both, -o, 1), 0.0)
    return out


def pick(places, values):
    return jnp.where(iota((128, 128), 0) & 63 == places, values, 0.0)


def picks(rank_a, rank_b, count):
    first = iota(rank_a.shape, 1) < 64
    low, high = jnp.minimum(rank_a, rank_b), jnp.maximum(rank_a, rank_b)
    couples = count * (count - 1) // 2
    place = ((low * (2 * count - 1 - low)) >> 1) + high - low - 1
    sign = jnp.where(first | (rank_a < rank_b), 1.0, -1.0)
    products = pick(place + jnp.where(first, 0, couples), sign)
    powers = pick(2 * couples + jnp.where(first, rank_a, rank_b), jnp.ones_like(sign))
    return products, powers


MESH = pl.DeviceIdType.MESH


def partner(me, m):
    out = 0
    for n in range(3):
        mine, other = me // 2**n % 2, m // 2**n % 2
        out = out + 2**n * (mine + other - 2 * mine * other)
    return out


def list_dates(pairs, dates, peers):
    length = pairs.shape[1]
    part = length // peers
    date = iota((dates, length), 0)
    named = (pairs[0:1] == date) | (pairs[1:2] == date)
    parts = iota((length, 128), 0) // part == iota((length, 128), 1)
    dims = (((1,), (0,)), ((), ()))
    one = jnp.bfloat16
    counts = lax.dot_general(
        named.astype(jnp.float32).astype(one),
        parts.astype(jnp.float32).astype(one),
        dims,
        preferred_element_type=jnp.float32,
    )
    needed = counts > 0.5
    before = iota((dates, dates), 1) < iota((dates, dates), 0)
    rank = lax.dot_general(
        before.astype(jnp.float32).astype(one),
        needed.astype(jnp.float32).astype(one),
        dims,
        preferred_element_type=jnp.float32,
    )
    rank = jnp.where(needed, rank, -1.0).astype(jnp.int32)
    date = iota(rank.shape, 0)
    rows = [jnp.sum(jnp.where(rank == k, date, 0), axis=0, keepdims=True) for k in range(peers)]
    return jnp.concatenate(rows, 0)


def stack_kernel(
    slc_ref,
    pairs_hbm,
    table,
    boxed_ref,
    chosen,
    lines,
    sent,
    held,
    full,
    sums,
    tiles,
    near_sums,
    near_tiles,
    listed,
    ids,
    pairs_ref,
    pairs_sem,
    line_sem,
    send_a,
    recv_a,
    send_b,
    recv_b,
    list_sem,
):
    peers, az_size = lax.axis_size("date"), lax.axis_size("az")
    me, az = lax.axis_index("date"), lax.axis_index("az")
    date_dev = slc_ref.shape[0]
    rounds = pairs_ref.shape[0]
    width = slc_ref.shape[3] // peers
    images_dev = 2 * date_dev
    sides = ((-1, az > 0), (1, az < az_size - 1))
    kinds = ((0, None),) + sides

    named = pltpu.make_async_copy(pairs_hbm, pairs_ref, pairs_sem)
    barrier = pltpu.get_barrier_semaphore()
    for n in range(date_dev):
        pltpu.make_async_copy(slc_ref.at[n], lines.at[n], line_sem).start()
    named.start()
    for o in range(1, peers):
        pl.semaphore_signal(
            barrier, inc=1, device_id={"date": lax.rem(me + o, peers)}, device_id_type=MESH
        )
    for step, there in sides:

        @pl.when(there)
        def _():
            pl.semaphore_signal(barrier, inc=1, device_id={"az": az + step}, device_id_type=MESH)

    rows_date = sent.shape[1] // date_dev
    pltpu.make_async_copy(slc_ref, lines, line_sem).wait()
    for n in range(date_dev):
        for j in range(peers):
            part = lines[n, :, :, j * width : (j + 1) * width]
            at = slice(n * rows_date, (n + 1) * rows_date)
            sent[j, at] = part.reshape(rows_date, width).astype(jnp.bfloat16)
    greeted = peers - 1 + (az > 0).astype(jnp.int32) + (az < az_size - 1).astype(jnp.int32)
    pl.semaphore_wait(barrier, greeted)

    def images(o):
        peer = partner(me, o)
        return pltpu.make_async_remote_copy(
            src_ref=sent.at[peer],
            dst_ref=held.at[me],
            send_sem=send_a,
            recv_sem=recv_a.at[o],
            device_id={"date": peer},
            device_id_type=MESH,
        )

    for o in range(peers - 1, 0, -1):
        images(o).start()
    named.wait()
    for r in range(rounds):
        listed[r * peers : (r + 1) * peers, :] = list_dates(
            pairs_ref[r], date_dev * peers, peers
        )
    fetch = pltpu.make_async_copy(listed, ids, list_sem)
    fetch.start()
    order = sample_order()

    def take(owner, block):
        spread = jnp.dot(block, order, preferred_element_type=jnp.float32)
        for image in range(images_dev):
            for group in range(2):
                row = image * 8 + group * LINES
                at = (owner * images_dev + image, pl.ds(group, LINES, stride=2))
                full[at] = spread[row : row + LINES]

    take(me, sent[me])
    fetch.wait()
    lane = iota((1, 128), 1)
    for r in range(rounds):
        ranks = []
        for c in range(2):
            start = pl.multiple_of(me // 2 * 128, 128)
            near = pairs_ref[r, c : c + 1, pl.ds(start, 128)]
            own = jnp.where((lane < 64) == (lax.rem(me, 2) == 0), near, rolled(near, 64, 1))
            rank = jnp.zeros_like(own)
            for k in range(peers):
                rank = rank + (own > ids[r * peers + k, me]).astype(jnp.int32)
            ranks.append(rank)
        products, powers = picks(*ranks, peers)
        chosen[r, :128, :] = products.T.astype(jnp.bfloat16)
        chosen[r, 128:, :] = powers.T.astype(jnp.bfloat16)
    for o in range(1, peers):
        images(o).wait_recv()
        owner = partner(me, o)
        take(owner, held[owner])

    def result(kind, peer):
        step, _ = kinds[kind]
        device = {"date": peer}
        if step:
            device["az"] = az + step
        return pltpu.make_async_remote_copy(
            src_ref=(near_sums.at[kind - 1] if kind else sums).at[peer],
            dst_ref=(near_tiles.at[kind - 1] if kind else tiles).at[me],
            send_sem=send_b.at[kind],
            recv_sem=recv_b.at[kind],
            device_id=device,
            device_id_type=MESH,
        )

    def serve(n, carry):
        m = peers - 1 - n
        peer = partner(me, m)
        shares = []
        for r in range(rounds):
            real, imag = [], []
            for k in range(peers):
                date = ids[r * peers + k, peer]
                real.append(full[2 * date])
                imag.append(full[2 * date + 1])
            shares.append(shares_of(cell_sums(real, imag)))
        for kind in range(3):
            share = jnp.concatenate([shares[r][kind] for r in range(rounds)], 0)
            if kind:
                near_sums[kind - 1, peer] = share.astype(jnp.bfloat16)
            else:
                sums[peer] = share
        for kind, (step, there) in enumerate(kinds):

            @pl.when(there if step else m > 0)
            def _():
                result(kind, peer).start()

        return carry

    for kind, (step, there) in enumerate(kinds):
        if step:

            @pl.when(jnp.logical_not(there))
            def _():
                near_tiles[2 - kind] = jnp.zeros_like(near_tiles[2 - kind])

    lax.fori_loop(0, peers, serve, 0)
    tiles[me] = sums[me]

    def all_of(src, dst, count, send_sem, recv_sem):
        part = pl.ds(0, count)
        return pltpu.make_async_remote_copy(
            src_ref=src.at[part],
            dst_ref=dst.at[part],
            send_sem=send_sem,
            recv_sem=recv_sem,
            device_id={"date": lax.rem(me + 1, peers)},
            device_id_type=MESH,
        )

    def all_results(kind):
        sems = send_b.at[kind], recv_b.at[kind]
        if kind:
            return all_of(near_sums.at[kind - 1], near_tiles.at[kind - 1], peers, *sems)
        return all_of(sums, tiles, peers - 1, *sems)

    all_results(0).wait_recv()
    for kind, (step, there) in enumerate(kinds):
        if step:

            @pl.when(there)
            def _():
                all_results(3 - kind).wait_recv()

    own, near = [], []
    for j in range(peers):
        own.append(tiles[j])
        sides_sum = near_tiles[0, j].astype(jnp.float32) + near_tiles[1, j].astype(jnp.float32)
        near.append(both_rows(own[-1]) + sides_sum)
    for r in range(rounds):
        at = slice(8 * r, 8 * r + 8)
        table[r] = jnp.concatenate(table_of([x[at] for x in own]), 0)
        boxed_ref[r] = box_of(jnp.concatenate(table_of([x[at] for x in near]), 0))

    all_of(sent, held, peers - 1, send_a, recv_a.at[0]).wait_send()
    all_results(0).wait_send()
    for kind, (step, there) in enumerate(kinds):
        if step:

            @pl.when(there)
            def _():
                all_results(kind).wait_send()


def pairs_kernel(table_ref, boxed_ref, chosen_ref, ifg_hbm, coh_hbm, ifg_ref, coh_ref, sems):
    rounds = table_ref.shape[0]

    def out(r, src, dst, n):
        rows = src.shape[0] // rounds
        at = pl.ds(rows * r, rows)
        return pltpu.make_async_copy(src.at[at], dst.at[at], sems.at[n, r])

    for r in range(rounds):
        means = jnp.dot(
            chosen_ref[r, :128], in_two(table_ref[r]), preferred_element_type=jnp.float32
        )
        for c in range(2):
            for row in range(2):
                part = means[64 * c : 64 * c + 64, 64 * row : 64 * row + 64]
                ifg_ref[pl.ds(256 * r + 2 * c + row, 64, stride=4), :] = part
        out(r, ifg_ref, ifg_hbm, 0).start()
        parts = jnp.dot(
            chosen_ref[r], in_two(boxed_ref[r]), preferred_element_type=jnp.float32
        )
        size = jnp.sqrt(parts[:64] * parts[:64] + parts[64:128] * parts[64:128])
        coherence = size / jnp.sqrt(parts[128:192] * parts[192:])
        for row in range(2):
            part = coherence[:, 64 * row : 64 * row + 64]
            coh_ref[pl.ds(128 * r + row, 64, stride=2), :] = part
        out(r, coh_ref, coh_hbm, 1).start()
    for r in range(rounds):
        out(r, ifg_ref, ifg_hbm, 0).wait()
        out(r, coh_ref, coh_hbm, 1).wait()


def per_device_few(slc, pairs):
    peers = lax.axis_size("date")
    rounds = pairs.shape[0]
    pair_dev = pairs.shape[1] // peers
    date_dev, _, lines, columns = slc.shape
    width = columns // peers
    rows = date_dev * 2 * lines
    cells = columns // SAMPLES
    vmem = pl.BlockSpec(memory_space=pltpu.VMEM)
    hbm = pl.BlockSpec(memory_space=pltpu.HBM)
    dma = pltpu.SemaphoreType.DMA
    found = pl.pallas_call(
        stack_kernel,
        out_shape=(
            jax.ShapeDtypeStruct((rounds, 64, 128), jnp.float32),
            jax.ShapeDtypeStruct((rounds, 64, 128), jnp.float32),
            jax.ShapeDtypeStruct((rounds, 256, 128), jnp.bfloat16),
        ),
        in_specs=[hbm, hbm],
        out_specs=(vmem,) * 3,
        scratch_shapes=[
            pltpu.VMEM(slc.shape, jnp.float32),
            pltpu.VMEM((peers, rows, width), jnp.bfloat16),
            pltpu.VMEM((peers, rows, width), jnp.bfloat16),
            pltpu.VMEM((peers * date_dev * 2, lines, width), jnp.float32),
            pltpu.VMEM((peers, rounds * 8, 128), jnp.float32),
            pltpu.VMEM((peers, rounds * 8, 128), jnp.float32),
            pltpu.VMEM((2, peers, rounds * 8, 128), jnp.bfloat16),
            pltpu.VMEM((2, peers, rounds * 8, 128), jnp.bfloat16),
            pltpu.VMEM((rounds * peers, 128), jnp.int32),
            pltpu.SMEM((rounds * peers, 128), jnp.int32),
            pltpu.VMEM((rounds, 2, pairs.shape[1]), jnp.int32),
            dma,
            dma,
            dma,
            dma((peers,)),
            dma((3,)),
            dma((3,)),
            dma,
        ],
        compiler_params=pltpu.CompilerParams(
            collective_id=0, has_side_effects=True, vmem_limit_bytes=VMEM_LIMIT
        ),
    )(
        pltpu.with_memory_space_constraint(slc, pltpu.HBM),
        pltpu.with_memory_space_constraint(pairs.transpose(0, 2, 1), pltpu.HBM),
    )
    ifg_shape = (rounds * pair_dev * 2 * lines // LINES, cells)
    coh_shape = (rounds * pair_dev * lines // LINES, cells)
    ifg, coh = pl.pallas_call(
        pairs_kernel,
        out_shape=(
            jax.ShapeDtypeStruct(ifg_shape, jnp.float32),
            jax.ShapeDtypeStruct(coh_shape, jnp.float32),
        ),
        in_specs=[vmem] * 3,
        out_specs=(hbm, hbm),
        scratch_shapes=[
            pltpu.VMEM(ifg_shape, jnp.float32),
            pltpu.VMEM(coh_shape, jnp.float32),
            dma((2, rounds)),
        ],
        compiler_params=pltpu.CompilerParams(vmem_limit_bytes=VMEM_LIMIT),
    )(*found)
    return (
        ifg.reshape(rounds, pair_dev, 2, lines // LINES, cells),
        coh.reshape(rounds, pair_dev, lines // LINES, cells),
    )


def per_device(slc, pairs):
    peers = lax.axis_size("date")
    lines, columns = slc.shape[2:]
    pair_dev = pairs.shape[1] // peers
    few = (peers, pair_dev, lines, columns) == (8, 64, 2 * LINES, 64 * SAMPLES)
    return per_device_few(slc, pairs) if few else per_device_general(slc, pairs)


def solution(mesh):
    return jax.shard_map(
        per_device,
        mesh=mesh,
        in_specs=(P("date", None, "az", None), P()),
        out_specs=(P(None, "date", None, "az", None), P(None, "date", "az", None)),
        check_vma=False,
    )
```

```python
import jax
import jax.numpy as jnp
from jax import lax
from jax.experimental import pallas as pl
from jax.experimental.pallas import tpu as pltpu
from jax.sharding import PartitionSpec as P

CAP = 2
VMEM_LIMIT = 4 << 20


def with_halo(shard, sides, width):
    for axis, dim in sides:
        peers, length = (lax.axis_size(axis), shard.shape[dim])
        up = [(i, (i + 1) % peers) for i in range(peers - 1)]
        down = [(j, i) for i, j in up]
        last = lax.slice_in_dim(shard, length - width, length, axis=dim)
        first = lax.slice_in_dim(shard, 0, width, axis=dim)
        before = lax.ppermute(last, axis, up)
        after = lax.ppermute(first, axis, down)
        shard = jnp.concatenate([before, shard, after], axis=dim)
    return shard


def multilook(field):
    shape = field.shape
    blocks = field.reshape(shape[:-2] + (shape[-2] // 4, 4, shape[-1] // 16, 16))
    return blocks.mean(axis=(-3, -1))


def pair_looks(tiles):
    first = tiles[:, 0].astype(jnp.float32)
    second = tiles[:, 1].astype(jnp.float32)
    first_re, first_im = (first[:, 0], first[:, 1])
    second_re, second_im = (second[:, 0], second[:, 1])
    prod_re = first_re * second_re + first_im * second_im
    prod_im = first_im * second_re - first_re * second_im
    power_a = first_re * first_re + first_im * first_im
    power_b = second_re * second_re + second_im * second_im
    return jnp.stack(
        [multilook(prod_re), multilook(prod_im), multilook(power_a), multilook(power_b)], axis=1
    )


def coherence_from(padded):
    lines = padded.shape[-2] - 4
    columns = padded.shape[-1]
    az_sum = padded[..., 0:lines, :]
    for offset in range(1, 5):
        az_sum = az_sum + padded[..., offset : offset + lines, :]
    widths = [(0, 0)] * (az_sum.ndim - 1) + [(2, 2)]
    wide = jnp.pad(az_sum, widths)
    boxed = wide[..., 0:columns]
    for offset in range(1, 5):
        boxed = boxed + wide[..., offset : offset + columns]
    numer = jnp.sqrt(boxed[..., 0, :, :] ** 2 + boxed[..., 1, :, :] ** 2)
    return numer / jnp.sqrt(boxed[..., 2, :, :] * boxed[..., 3, :, :])


def per_device_general(slc, pairs):
    date_count = lax.axis_size("date")
    own_index = lax.axis_index("date")
    date_dev = slc.shape[0]
    pair_dev = pairs.shape[1] // date_count
    tile_shape = slc.shape[1:]
    quantized = lax.optimization_barrier(slc.astype(jnp.bfloat16))
    all_ids = jnp.arange(date_count * date_dev, dtype=jnp.int32)
    local_ids = own_index * date_dev + jnp.arange(date_dev, dtype=jnp.int32)
    local_pos = jnp.arange(date_dev, dtype=jnp.int32)
    slot_ids = jnp.arange(CAP, dtype=jnp.int32)
    looks_list = []
    for round_index in range(pairs.shape[0]):
        block = pairs[round_index]
        own_pairs = lax.dynamic_slice_in_dim(block, own_index * pair_dev, pair_dev, 0)
        entries = own_pairs.reshape(-1)
        wanted = block.reshape(date_count, 2 * pair_dev)
        needed = jnp.any(wanted[:, :, None] == local_ids[None, None, :], axis=1).astype(jnp.int32)
        ranks = jnp.cumsum(needed, axis=1) - needed
        picked = needed[:, None, :] * (ranks[:, None, :] == slot_ids[None, :, None]).astype(
            jnp.int32
        )
        source_local = jnp.sum(picked * local_pos[None, None, :], axis=2)
        present = jnp.sum(picked, axis=2) > 0
        outgoing = jnp.take(quantized, source_local.reshape(-1), axis=0).reshape(
            (date_count, CAP) + tile_shape
        )
        outgoing = jnp.where(present[:, :, None, None, None], outgoing, jnp.zeros((), jnp.bfloat16))
        incoming = lax.all_to_all(outgoing, "date", split_axis=0, concat_axis=0, tiled=True)
        matches = entries[:, None] == all_ids[None, :]
        my_need = jnp.any(matches, axis=0).astype(jnp.int32).reshape(date_count, date_dev)
        my_rank = (jnp.cumsum(my_need, axis=1) - my_need).reshape(-1)
        entry_slot = jnp.sum(jnp.where(matches, my_rank[None, :], 0), axis=1)
        position = entries // date_dev * CAP + entry_slot
        fetched = jnp.take(incoming.reshape((date_count * CAP,) + tile_shape), position, axis=0)
        looks = pair_looks(fetched.reshape((pair_dev, 2) + tile_shape))
        looks_list.append(looks)
    stacked = jnp.stack(looks_list, axis=0)
    padded = with_halo(stacked, (("az", 3),), 2)
    coherence = coherence_from(padded)
    interferogram = stacked[:, :, 0:2]
    return (interferogram, coherence)


LINES, SAMPLES = 4, 16
STEPS = ((0, 2, 2), (0, 2, 1), (1, 8, 8), (1, 8, 4), (1, 8, 2), (1, 8, 1))


def iota(shape, dim):
    return lax.broadcasted_iota(jnp.int32, shape, dim)


def place_of(leaf):
    bit = [(leaf >> n) & 1 for n in range(6)]
    return 32 * bit[3] + 16 * bit[4] + 8 * bit[5] + 4 * bit[0] + 2 * bit[1] + bit[2]


def rolled(x, shift, dim):
    return pltpu.roll(x, shift % x.shape[dim], dim)


def join(one, two, dim, unit, dist, phase):
    low = ((iota(one.shape, dim) - unit * phase) & (unit * dist)) == 0
    kept = jnp.where(low, one, two)
    other = jnp.where(low, two, one)
    return kept + rolled(other, -unit * dist, dim)


def cell_sums(real, imag):
    count = len(real)
    couples = [(i, j) for i in range(count) for j in range(i + 1, count)]

    def quantity(place):
        if place < len(couples):
            i, j = couples[place]
            return real[i] * real[j] + imag[i] * imag[j]
        place -= len(couples)
        if place < len(couples):
            i, j = couples[place]
            return imag[i] * real[j] - real[i] * imag[j]
        i = place - len(couples)
        return real[i] * real[i] + imag[i] * imag[i]

    def build(level, base, phases):
        if level == 0:
            return quantity(place_of(base))
        dim, unit, dist = STEPS[level - 1]
        moved = tuple(p + dist if d == dim else p for d, p in enumerate(phases))
        one = build(level - 1, base, phases)
        two = build(level - 1, base + (1 << (level - 1)), moved)
        return join(one, two, dim, unit, dist, phases[dim])

    return build(len(STEPS), 0, (0, 0))


def in_two(x):
    high = x.astype(jnp.bfloat16)
    low = (x - high.astype(jnp.float32)).astype(jnp.bfloat16)
    return jnp.concatenate([high, low], 0)


def sample_order():
    src, dst = iota((128, 128), 0), iota((128, 128), 1)
    hit = dst == (src % SAMPLES) * (128 // SAMPLES) + src // SAMPLES
    return jnp.where(hit, 1.0 / 8, 0.0).astype(jnp.bfloat16)


def table_of(tiles):
    lane, sub = iota((8, 128), 1), iota((8, 128), 0)
    tiles = list(tiles)
    for b in range(3):
        dist = 8 << b
        low = (lane & dist) == 0
        for j in range(8):
            if not j >> b & 1:
                one, two = tiles[j], tiles[j | 1 << b]
                tiles[j] = jnp.where(low, one, rolled(two, dist, 1))
                tiles[j | 1 << b] = jnp.where(low, rolled(one, -dist, 1), two)
    even, first = (sub & 1) == 0, lane < 64
    out = []
    for tile in tiles:
        far = rolled(tile, 64, 1)
        moved = jnp.where(even, rolled(far, -1, 0), rolled(far, 1, 0))
        out.append(jnp.where(even == first, tile, moved))
    return out


def both_rows(x):
    odd = (iota(x.shape, 0) & 1) == 1
    return x + jnp.where(odd, rolled(x, 1, 0), rolled(x, -1, 0))


def shares_of(x):
    odd = (iota(x.shape, 0) & 1) == 1
    both = both_rows(x)
    return x, jnp.where(odd, both, x), jnp.where(odd, x, both)


def box_of(both):
    cell = iota(both.shape, 1) & 63
    out = both
    for o in (-2, -1, 1, 2):
        valid = (cell + o >= 0) & (cell + o < 64)
        out = out + jnp.where(valid, rolled(both, -o, 1), 0.0)
    return out


def pick(places, values):
    return jnp.where(iota((128, 128), 0) & 63 == places, values, 0.0)


def picks(rank_a, rank_b, count):
    first = iota(rank_a.shape, 1) < 64
    low, high = jnp.minimum(rank_a, rank_b), jnp.maximum(rank_a, rank_b)
    couples = count * (count - 1) // 2
    place = ((low * (2 * count - 1 - low)) >> 1) + high - low - 1
    sign = jnp.where(first | (rank_a < rank_b), 1.0, -1.0)
    products = pick(place + jnp.where(first, 0, couples), sign)
    powers = pick(2 * couples + jnp.where(first, rank_a, rank_b), jnp.ones_like(sign))
    return products, powers


MESH = pl.DeviceIdType.MESH


def partner(me, m):
    out = 0
    for n in range(3):
        mine, other = me // 2**n % 2, m // 2**n % 2
        out = out + 2**n * (mine + other - 2 * mine * other)
    return out


def list_dates(pairs, dates, peers):
    length = pairs.shape[1]
    part = length // peers
    date = iota((dates, length), 0)
    named = (pairs[0:1] == date) | (pairs[1:2] == date)
    parts = iota((length, 128), 0) // part == iota((length, 128), 1)
    dims = (((1,), (0,)), ((), ()))
    one = jnp.bfloat16
    counts = lax.dot_general(
        named.astype(jnp.float32).astype(one),
        parts.astype(jnp.float32).astype(one),
        dims,
        preferred_element_type=jnp.float32,
    )
    needed = counts > 0.5
    before = iota((dates, dates), 1) < iota((dates, dates), 0)
    rank = lax.dot_general(
        before.astype(jnp.float32).astype(one),
        needed.astype(jnp.float32).astype(one),
        dims,
        preferred_element_type=jnp.float32,
    )
    rank = jnp.where(needed, rank, -1.0).astype(jnp.int32)
    date = iota(rank.shape, 0)
    rows = [jnp.sum(jnp.where(rank == k, date, 0), axis=0, keepdims=True) for k in range(peers)]
    return jnp.concatenate(rows, 0)


def stack_kernel(
    slc_ref,
    pairs_hbm,
    table,
    boxed_ref,
    chosen,
    lines,
    sent,
    held,
    full,
    sums,
    tiles,
    near_sums,
    near_tiles,
    listed,
    ids,
    pairs_ref,
    pairs_sem,
    line_sem,
    send_a,
    recv_a,
    send_b,
    recv_b,
    list_sem,
    known,
):
    peers, az_size = lax.axis_size("date"), lax.axis_size("az")
    me, az = lax.axis_index("date"), lax.axis_index("az")
    date_dev = slc_ref.shape[0]
    rounds = pairs_ref.shape[0]
    width = slc_ref.shape[3] // peers
    images_dev = 2 * date_dev
    sides = ((-1, az > 0), (1, az < az_size - 1))
    kinds = ((0, None),) + sides

    named = pltpu.make_async_copy(pairs_hbm, pairs_ref, pairs_sem)
    barrier = pltpu.get_barrier_semaphore()
    for n in range(date_dev):
        pltpu.make_async_copy(slc_ref.at[n], lines.at[n], line_sem).start()
    named.start()
    across = lax.rem(me, 2)
    along = me // 2
    depth = peers // 2
    beside = me + 1 - 2 * across

    def greet(sem):
        pl.semaphore_signal(sem, inc=1, device_id={"date": beside}, device_id_type=MESH)
        for step, there in ((-1, along > 0), (1, along < depth - 1)):

            @pl.when(there)
            def _():
                pl.semaphore_signal(
                    sem, inc=1, device_id={"date": me + 2 * step}, device_id_type=MESH
                )

    greet(barrier)
    for step, there in sides:

        @pl.when(there)
        def _():
            pl.semaphore_signal(barrier, inc=1, device_id={"az": az + step}, device_id_type=MESH)

    rows_date = sent.shape[1] // date_dev
    pltpu.make_async_copy(slc_ref, lines, line_sem).wait()
    for n in range(date_dev):
        for j in range(peers):
            part = lines[n, :, :, j * width : (j + 1) * width]
            at = slice(n * rows_date, (n + 1) * rows_date)
            sent[j, at] = part.reshape(rows_date, width).astype(jnp.bfloat16)
    close = 1 + (along > 0).astype(jnp.int32) + (along < depth - 1).astype(jnp.int32)
    lines_near = (az > 0).astype(jnp.int32) + (az < az_size - 1).astype(jnp.int32)
    pl.semaphore_wait(barrier, close + lines_near)

    def images(peer):
        return pltpu.make_async_remote_copy(
            src_ref=sent.at[peer],
            dst_ref=held.at[me],
            send_sem=send_a,
            recv_sem=recv_a.at[me],
            device_id={"date": peer},
            device_id_type=MESH,
        )

    def tell(sem, step, there):
        @pl.when(there)
        def _():
            pl.semaphore_signal(
                sem, inc=1, device_id={"date": me + 2 * step}, device_id_type=MESH
            )

    def send(column, step):
        @pl.when((along + step >= 0) & (along + step < depth))
        def _():
            images(column + 2 * step).start()

    for way in (-1, 1):
        tell(known.at[(way + 1) // 2, 0], way, (along + way >= 0) & (along + way < depth))
    for way in (1, -1):
        send(me, way)
    images(beside).start()
    for hops in range(1, depth):
        for way in (1, -1):
            news = known.at[(way + 1) // 2]

            @pl.when((along - way * hops >= 0) & (along - way * hops < depth))
            def _():
                pl.semaphore_wait(news.at[hops - 1], 1)
                if hops < depth - 1:
                    tell(news.at[hops], way, (along + way >= 0) & (along + way < depth))
                send(me, -way * (hops + 1))
                send(beside, -way * hops)

    named.wait()
    for r in range(rounds):
        listed[r * peers : (r + 1) * peers, :] = list_dates(
            pairs_ref[r], date_dev * peers, peers
        )
    fetch = pltpu.make_async_copy(listed, ids, list_sem)
    fetch.start()
    order = sample_order()

    def take(owner, block):
        spread = jnp.dot(block, order, preferred_element_type=jnp.float32)
        for image in range(images_dev):
            for group in range(2):
                row = image * 8 + group * LINES
                at = (owner * images_dev + image, pl.ds(group, LINES, stride=2))
                full[at] = spread[row : row + LINES]

    take(me, sent[me])
    fetch.wait()
    lane = iota((1, 128), 1)
    for r in range(rounds):
        ranks = []
        for c in range(2):
            start = pl.multiple_of(me // 2 * 128, 128)
            near = pairs_ref[r, c : c + 1, pl.ds(start, 128)]
            own = jnp.where((lane < 64) == (lax.rem(me, 2) == 0), near, rolled(near, 64, 1))
            rank = jnp.zeros_like(own)
            for k in range(peers):
                rank = rank + (own > ids[r * peers + k, me]).astype(jnp.int32)
            ranks.append(rank)
        products, powers = picks(*ranks, peers)
        chosen[r, :128, :] = products.T.astype(jnp.bfloat16)
        chosen[r, 128:, :] = powers.T.astype(jnp.bfloat16)
    def arrival(owner):
        return pltpu.make_async_remote_copy(
            src_ref=sent.at[owner],
            dst_ref=held.at[owner],
            send_sem=send_a,
            recv_sem=recv_a.at[owner],
            device_id={"date": owner},
            device_id_type=MESH,
        )

    for o in range(1, peers):
        owner = partner(me, o)
        arrival(owner).wait_recv()
        take(owner, held[owner])

    def result(kind, peer):
        step, _ = kinds[kind]
        device = {"date": peer}
        if step:
            device["az"] = az + step
        return pltpu.make_async_remote_copy(
            src_ref=(near_sums.at[kind - 1] if kind else sums).at[peer],
            dst_ref=(near_tiles.at[kind - 1] if kind else tiles).at[me],
            send_sem=send_b.at[kind],
            recv_sem=recv_b.at[kind],
            device_id=device,
            device_id_type=MESH,
        )

    def serve(peer, carry):
        shares = []
        for r in range(rounds):
            real, imag = [], []
            for k in range(peers):
                date = ids[r * peers + k, peer]
                real.append(full[2 * date])
                imag.append(full[2 * date + 1])
            shares.append(shares_of(cell_sums(real, imag)))
        for kind in range(3):
            share = jnp.concatenate([shares[r][kind] for r in range(rounds)], 0)
            if kind:
                near_sums[kind - 1, peer] = share.astype(jnp.bfloat16)
            else:
                sums[peer] = share
        for kind, (step, there) in enumerate(kinds):

            @pl.when(there if step else peer != me)
            def _():
                result(kind, peer).start()

        return carry

    for kind, (step, there) in enumerate(kinds):
        if step:

            @pl.when(jnp.logical_not(there))
            def _():
                near_tiles[2 - kind] = jnp.zeros_like(near_tiles[2 - kind])

    lax.fori_loop(0, peers, serve, 0)
    tiles[me] = sums[me]

    def all_of(src, dst, count, send_sem, recv_sem):
        part = pl.ds(0, count)
        return pltpu.make_async_remote_copy(
            src_ref=src.at[part],
            dst_ref=dst.at[part],
            send_sem=send_sem,
            recv_sem=recv_sem,
            device_id={"date": lax.rem(me + 1, peers)},
            device_id_type=MESH,
        )

    def all_results(kind):
        sems = send_b.at[kind], recv_b.at[kind]
        if kind:
            return all_of(near_sums.at[kind - 1], near_tiles.at[kind - 1], peers, *sems)
        return all_of(sums, tiles, peers - 1, *sems)

    all_results(0).wait_recv()
    for kind, (step, there) in enumerate(kinds):
        if step:

            @pl.when(there)
            def _():
                all_results(3 - kind).wait_recv()

    own, near = [], []
    for j in range(peers):
        own.append(tiles[j])
        sides_sum = near_tiles[0, j].astype(jnp.float32) + near_tiles[1, j].astype(jnp.float32)
        near.append(both_rows(own[-1]) + sides_sum)
    for r in range(rounds):
        at = slice(8 * r, 8 * r + 8)
        table[r] = jnp.concatenate(table_of([x[at] for x in own]), 0)
        boxed_ref[r] = box_of(jnp.concatenate(table_of([x[at] for x in near]), 0))

    all_of(sent, held, peers - 1, send_a, recv_a.at[0]).wait_send()
    all_results(0).wait_send()
    for kind, (step, there) in enumerate(kinds):
        if step:

            @pl.when(there)
            def _():
                all_results(kind).wait_send()


def pairs_kernel(table_ref, boxed_ref, chosen_ref, ifg_hbm, coh_hbm, ifg_ref, coh_ref, sems):
    rounds = table_ref.shape[0]

    def out(r, src, dst, n):
        rows = src.shape[0] // rounds
        at = pl.ds(rows * r, rows)
        return pltpu.make_async_copy(src.at[at], dst.at[at], sems.at[n, r])

    for r in range(rounds):
        means = jnp.dot(
            chosen_ref[r, :128], in_two(table_ref[r]), preferred_element_type=jnp.float32
        )
        for c in range(2):
            for row in range(2):
                part = means[64 * c : 64 * c + 64, 64 * row : 64 * row + 64]
                ifg_ref[pl.ds(256 * r + 2 * c + row, 64, stride=4), :] = part
        out(r, ifg_ref, ifg_hbm, 0).start()
        parts = jnp.dot(
            chosen_ref[r], in_two(boxed_ref[r]), preferred_element_type=jnp.float32
        )
        size = jnp.sqrt(parts[:64] * parts[:64] + parts[64:128] * parts[64:128])
        coherence = size / jnp.sqrt(parts[128:192] * parts[192:])
        for row in range(2):
            part = coherence[:, 64 * row : 64 * row + 64]
            coh_ref[pl.ds(128 * r + row, 64, stride=2), :] = part
        out(r, coh_ref, coh_hbm, 1).start()
    for r in range(rounds):
        out(r, ifg_ref, ifg_hbm, 0).wait()
        out(r, coh_ref, coh_hbm, 1).wait()


def per_device_few(slc, pairs):
    peers = lax.axis_size("date")
    rounds = pairs.shape[0]
    pair_dev = pairs.shape[1] // peers
    date_dev, _, lines, columns = slc.shape
    width = columns // peers
    rows = date_dev * 2 * lines
    cells = columns // SAMPLES
    vmem = pl.BlockSpec(memory_space=pltpu.VMEM)
    hbm = pl.BlockSpec(memory_space=pltpu.HBM)
    dma = pltpu.SemaphoreType.DMA
    found = pl.pallas_call(
        stack_kernel,
        out_shape=(
            jax.ShapeDtypeStruct((rounds, 64, 128), jnp.float32),
            jax.ShapeDtypeStruct((rounds, 64, 128), jnp.float32),
            jax.ShapeDtypeStruct((rounds, 256, 128), jnp.bfloat16),
        ),
        in_specs=[hbm, hbm],
        out_specs=(vmem,) * 3,
        scratch_shapes=[
            pltpu.VMEM(slc.shape, jnp.float32),
            pltpu.VMEM((peers, rows, width), jnp.bfloat16),
            pltpu.VMEM((peers, rows, width), jnp.bfloat16),
            pltpu.VMEM((peers * date_dev * 2, lines, width), jnp.float32),
            pltpu.VMEM((peers, rounds * 8, 128), jnp.float32),
            pltpu.VMEM((peers, rounds * 8, 128), jnp.float32),
            pltpu.VMEM((2, peers, rounds * 8, 128), jnp.bfloat16),
            pltpu.VMEM((2, peers, rounds * 8, 128), jnp.bfloat16),
            pltpu.VMEM((rounds * peers, 128), jnp.int32),
            pltpu.SMEM((rounds * peers, 128), jnp.int32),
            pltpu.VMEM((rounds, 2, pairs.shape[1]), jnp.int32),
            dma,
            dma,
            dma,
            dma((peers,)),
            dma((3,)),
            dma((3,)),
            dma,
            pltpu.SemaphoreType.REGULAR((2, peers // 2 - 1)),
        ],
        compiler_params=pltpu.CompilerParams(
            collective_id=0, has_side_effects=True, vmem_limit_bytes=VMEM_LIMIT
        ),
    )(
        pltpu.with_memory_space_constraint(slc, pltpu.HBM),
        pltpu.with_memory_space_constraint(pairs.transpose(0, 2, 1), pltpu.HBM),
    )
    ifg_shape = (rounds * pair_dev * 2 * lines // LINES, cells)
    coh_shape = (rounds * pair_dev * lines // LINES, cells)
    ifg, coh = pl.pallas_call(
        pairs_kernel,
        out_shape=(
            jax.ShapeDtypeStruct(ifg_shape, jnp.float32),
            jax.ShapeDtypeStruct(coh_shape, jnp.float32),
        ),
        in_specs=[vmem] * 3,
        out_specs=(hbm, hbm),
        scratch_shapes=[
            pltpu.VMEM(ifg_shape, jnp.float32),
            pltpu.VMEM(coh_shape, jnp.float32),
            dma((2, rounds)),
        ],
        compiler_params=pltpu.CompilerParams(vmem_limit_bytes=VMEM_LIMIT),
    )(*found)
    return (
        ifg.reshape(rounds, pair_dev, 2, lines // LINES, cells),
        coh.reshape(rounds, pair_dev, lines // LINES, cells),
    )


def per_device(slc, pairs):
    peers = lax.axis_size("date")
    lines, columns = slc.shape[2:]
    pair_dev = pairs.shape[1] // peers
    few = (peers, pair_dev, lines, columns) == (8, 64, 2 * LINES, 64 * SAMPLES)
    return per_device_few(slc, pairs) if few else per_device_general(slc, pairs)


def solution(mesh):
    return jax.shard_map(
        per_device,
        mesh=mesh,
        in_specs=(P("date", None, "az", None), P()),
        out_specs=(P(None, "date", None, "az", None), P(None, "date", "az", None)),
        check_vma=False,
    )
```

```python
import jax
import jax.numpy as jnp
from jax import lax
from jax.experimental import pallas as pl
from jax.experimental.pallas import tpu as pltpu
from jax.sharding import PartitionSpec as P

CAP = 2
FAR_FIRST = (7, 5, 6, 3, 4, 2, 1)
VMEM_LIMIT = 4 << 20


def with_halo(shard, sides, width):
    for axis, dim in sides:
        peers, length = (lax.axis_size(axis), shard.shape[dim])
        up = [(i, (i + 1) % peers) for i in range(peers - 1)]
        down = [(j, i) for i, j in up]
        last = lax.slice_in_dim(shard, length - width, length, axis=dim)
        first = lax.slice_in_dim(shard, 0, width, axis=dim)
        before = lax.ppermute(last, axis, up)
        after = lax.ppermute(first, axis, down)
        shard = jnp.concatenate([before, shard, after], axis=dim)
    return shard


def multilook(field):
    shape = field.shape
    blocks = field.reshape(shape[:-2] + (shape[-2] // 4, 4, shape[-1] // 16, 16))
    return blocks.mean(axis=(-3, -1))


def pair_looks(tiles):
    first = tiles[:, 0].astype(jnp.float32)
    second = tiles[:, 1].astype(jnp.float32)
    first_re, first_im = (first[:, 0], first[:, 1])
    second_re, second_im = (second[:, 0], second[:, 1])
    prod_re = first_re * second_re + first_im * second_im
    prod_im = first_im * second_re - first_re * second_im
    power_a = first_re * first_re + first_im * first_im
    power_b = second_re * second_re + second_im * second_im
    return jnp.stack(
        [multilook(prod_re), multilook(prod_im), multilook(power_a), multilook(power_b)], axis=1
    )


def coherence_from(padded):
    lines = padded.shape[-2] - 4
    columns = padded.shape[-1]
    az_sum = padded[..., 0:lines, :]
    for offset in range(1, 5):
        az_sum = az_sum + padded[..., offset : offset + lines, :]
    widths = [(0, 0)] * (az_sum.ndim - 1) + [(2, 2)]
    wide = jnp.pad(az_sum, widths)
    boxed = wide[..., 0:columns]
    for offset in range(1, 5):
        boxed = boxed + wide[..., offset : offset + columns]
    numer = jnp.sqrt(boxed[..., 0, :, :] ** 2 + boxed[..., 1, :, :] ** 2)
    return numer / jnp.sqrt(boxed[..., 2, :, :] * boxed[..., 3, :, :])


def per_device_general(slc, pairs):
    date_count = lax.axis_size("date")
    own_index = lax.axis_index("date")
    date_dev = slc.shape[0]
    pair_dev = pairs.shape[1] // date_count
    tile_shape = slc.shape[1:]
    quantized = lax.optimization_barrier(slc.astype(jnp.bfloat16))
    all_ids = jnp.arange(date_count * date_dev, dtype=jnp.int32)
    local_ids = own_index * date_dev + jnp.arange(date_dev, dtype=jnp.int32)
    local_pos = jnp.arange(date_dev, dtype=jnp.int32)
    slot_ids = jnp.arange(CAP, dtype=jnp.int32)
    looks_list = []
    for round_index in range(pairs.shape[0]):
        block = pairs[round_index]
        own_pairs = lax.dynamic_slice_in_dim(block, own_index * pair_dev, pair_dev, 0)
        entries = own_pairs.reshape(-1)
        wanted = block.reshape(date_count, 2 * pair_dev)
        needed = jnp.any(wanted[:, :, None] == local_ids[None, None, :], axis=1).astype(jnp.int32)
        ranks = jnp.cumsum(needed, axis=1) - needed
        picked = needed[:, None, :] * (ranks[:, None, :] == slot_ids[None, :, None]).astype(
            jnp.int32
        )
        source_local = jnp.sum(picked * local_pos[None, None, :], axis=2)
        present = jnp.sum(picked, axis=2) > 0
        outgoing = jnp.take(quantized, source_local.reshape(-1), axis=0).reshape(
            (date_count, CAP) + tile_shape
        )
        outgoing = jnp.where(present[:, :, None, None, None], outgoing, jnp.zeros((), jnp.bfloat16))
        incoming = lax.all_to_all(outgoing, "date", split_axis=0, concat_axis=0, tiled=True)
        matches = entries[:, None] == all_ids[None, :]
        my_need = jnp.any(matches, axis=0).astype(jnp.int32).reshape(date_count, date_dev)
        my_rank = (jnp.cumsum(my_need, axis=1) - my_need).reshape(-1)
        entry_slot = jnp.sum(jnp.where(matches, my_rank[None, :], 0), axis=1)
        position = entries // date_dev * CAP + entry_slot
        fetched = jnp.take(incoming.reshape((date_count * CAP,) + tile_shape), position, axis=0)
        looks = pair_looks(fetched.reshape((pair_dev, 2) + tile_shape))
        looks_list.append(looks)
    stacked = jnp.stack(looks_list, axis=0)
    padded = with_halo(stacked, (("az", 3),), 2)
    coherence = coherence_from(padded)
    interferogram = stacked[:, :, 0:2]
    return (interferogram, coherence)


LINES, SAMPLES = 4, 16
STEPS = ((0, 2, 2), (0, 2, 1), (1, 8, 8), (1, 8, 4), (1, 8, 2), (1, 8, 1))


def iota(shape, dim):
    return lax.broadcasted_iota(jnp.int32, shape, dim)


def place_of(leaf):
    bit = [(leaf >> n) & 1 for n in range(6)]
    return 32 * bit[3] + 16 * bit[4] + 8 * bit[5] + 4 * bit[0] + 2 * bit[1] + bit[2]


def rolled(x, shift, dim):
    return pltpu.roll(x, shift % x.shape[dim], dim)


def join(one, two, dim, unit, dist, phase):
    low = ((iota(one.shape, dim) - unit * phase) & (unit * dist)) == 0
    kept = jnp.where(low, one, two)
    other = jnp.where(low, two, one)
    return kept + rolled(other, -unit * dist, dim)


def cell_sums(real, imag):
    count = len(real)
    couples = [(i, j) for i in range(count) for j in range(i + 1, count)]

    def quantity(place):
        if place < len(couples):
            i, j = couples[place]
            return real[i] * real[j] + imag[i] * imag[j]
        place -= len(couples)
        if place < len(couples):
            i, j = couples[place]
            return imag[i] * real[j] - real[i] * imag[j]
        i = place - len(couples)
        return real[i] * real[i] + imag[i] * imag[i]

    def build(level, base, phases):
        if level == 0:
            return quantity(place_of(base))
        dim, unit, dist = STEPS[level - 1]
        moved = tuple(p + dist if d == dim else p for d, p in enumerate(phases))
        one = build(level - 1, base, phases)
        two = build(level - 1, base + (1 << (level - 1)), moved)
        return join(one, two, dim, unit, dist, phases[dim])

    return build(len(STEPS), 0, (0, 0))


def in_two(x):
    high = x.astype(jnp.bfloat16)
    low = (x - high.astype(jnp.float32)).astype(jnp.bfloat16)
    return jnp.concatenate([high, low], 0)


def sample_order():
    src, dst = iota((128, 128), 0), iota((128, 128), 1)
    hit = dst == (src % SAMPLES) * (128 // SAMPLES) + src // SAMPLES
    return jnp.where(hit, 1.0 / 8, 0.0).astype(jnp.bfloat16)


def table_of(tiles):
    lane, sub = iota((8, 128), 1), iota((8, 128), 0)
    tiles = list(tiles)
    for b in range(3):
        dist = 8 << b
        low = (lane & dist) == 0
        for j in range(8):
            if not j >> b & 1:
                one, two = tiles[j], tiles[j | 1 << b]
                tiles[j] = jnp.where(low, one, rolled(two, dist, 1))
                tiles[j | 1 << b] = jnp.where(low, rolled(one, -dist, 1), two)
    even, first = (sub & 1) == 0, lane < 64
    out = []
    for tile in tiles:
        far = rolled(tile, 64, 1)
        moved = jnp.where(even, rolled(far, -1, 0), rolled(far, 1, 0))
        out.append(jnp.where(even == first, tile, moved))
    return out


def both_rows(x):
    odd = (iota(x.shape, 0) & 1) == 1
    return x + jnp.where(odd, rolled(x, 1, 0), rolled(x, -1, 0))


def shares_of(x):
    odd = (iota(x.shape, 0) & 1) == 1
    both = both_rows(x)
    return x, jnp.where(odd, both, x), jnp.where(odd, x, both)


def box_of(both):
    cell = iota(both.shape, 1) & 63
    out = both
    for o in (-2, -1, 1, 2):
        valid = (cell + o >= 0) & (cell + o < 64)
        out = out + jnp.where(valid, rolled(both, -o, 1), 0.0)
    return out


def pick(places, values):
    return jnp.where(iota((128, 128), 0) & 63 == places, values, 0.0)


def picks(rank_a, rank_b, count):
    first = iota(rank_a.shape, 1) < 64
    low, high = jnp.minimum(rank_a, rank_b), jnp.maximum(rank_a, rank_b)
    couples = count * (count - 1) // 2
    place = ((low * (2 * count - 1 - low)) >> 1) + high - low - 1
    sign = jnp.where(first | (rank_a < rank_b), 1.0, -1.0)
    products = pick(place + jnp.where(first, 0, couples), sign)
    powers = pick(2 * couples + jnp.where(first, rank_a, rank_b), jnp.ones_like(sign))
    return products, powers


MESH = pl.DeviceIdType.MESH


def partner(me, m):
    out = 0
    for n in range(3):
        mine, other = me // 2**n % 2, m // 2**n % 2
        out = out + 2**n * (mine + other - 2 * mine * other)
    return out


def list_dates(pairs, dates, peers):
    length = pairs.shape[1]
    part = length // peers
    date = iota((dates, length), 0)
    named = (pairs[0:1] == date) | (pairs[1:2] == date)
    parts = iota((length, 128), 0) // part == iota((length, 128), 1)
    dims = (((1,), (0,)), ((), ()))
    one = jnp.bfloat16
    counts = lax.dot_general(
        named.astype(jnp.float32).astype(one),
        parts.astype(jnp.float32).astype(one),
        dims,
        preferred_element_type=jnp.float32,
    )
    needed = counts > 0.5
    before = iota((dates, dates), 1) < iota((dates, dates), 0)
    rank = lax.dot_general(
        before.astype(jnp.float32).astype(one),
        needed.astype(jnp.float32).astype(one),
        dims,
        preferred_element_type=jnp.float32,
    )
    rank = jnp.where(needed, rank, -1.0).astype(jnp.int32)
    date = iota(rank.shape, 0)
    rows = [jnp.sum(jnp.where(rank == k, date, 0), axis=0, keepdims=True) for k in range(peers)]
    return jnp.concatenate(rows, 0)


def stack_kernel(
    slc_ref,
    pairs_hbm,
    table,
    boxed_ref,
    chosen,
    lines,
    sent,
    held,
    full,
    sums,
    tiles,
    near_sums,
    near_tiles,
    listed,
    ids,
    pairs_ref,
    pairs_sem,
    line_sem,
    send_a,
    recv_a,
    send_b,
    recv_b,
    list_sem,
):
    peers, az_size = lax.axis_size("date"), lax.axis_size("az")
    me, az = lax.axis_index("date"), lax.axis_index("az")
    date_dev = slc_ref.shape[0]
    rounds = pairs_ref.shape[0]
    width = slc_ref.shape[3] // peers
    images_dev = 2 * date_dev
    sides = ((-1, az > 0), (1, az < az_size - 1))
    kinds = ((0, None),) + sides

    named = pltpu.make_async_copy(pairs_hbm, pairs_ref, pairs_sem)
    barrier = pltpu.get_barrier_semaphore()
    for n in range(date_dev):
        pltpu.make_async_copy(slc_ref.at[n], lines.at[n], line_sem).start()
    named.start()
    for o in range(1, peers):
        pl.semaphore_signal(
            barrier, inc=1, device_id={"date": lax.rem(me + o, peers)}, device_id_type=MESH
        )
    for step, there in sides:

        @pl.when(there)
        def _():
            pl.semaphore_signal(barrier, inc=1, device_id={"az": az + step}, device_id_type=MESH)

    rows_date = sent.shape[1] // date_dev
    pltpu.make_async_copy(slc_ref, lines, line_sem).wait()
    for n in range(date_dev):
        for j in range(peers):
            part = lines[n, :, :, j * width : (j + 1) * width]
            at = slice(n * rows_date, (n + 1) * rows_date)
            sent[j, at] = part.reshape(rows_date, width).astype(jnp.bfloat16)
    greeted = peers - 1 + (az > 0).astype(jnp.int32) + (az < az_size - 1).astype(jnp.int32)
    pl.semaphore_wait(barrier, greeted)

    def images(o):
        peer = partner(me, o)
        return pltpu.make_async_remote_copy(
            src_ref=sent.at[peer],
            dst_ref=held.at[me],
            send_sem=send_a,
            recv_sem=recv_a.at[o],
            device_id={"date": peer},
            device_id_type=MESH,
        )

    for o in FAR_FIRST:
        images(o).start()
    named.wait()
    for r in range(rounds):
        listed[r * peers : (r + 1) * peers, :] = list_dates(
            pairs_ref[r], date_dev * peers, peers
        )
    fetch = pltpu.make_async_copy(listed, ids, list_sem)
    fetch.start()
    order = sample_order()

    def take(owner, block):
        spread = jnp.dot(block, order, preferred_element_type=jnp.float32)
        for image in range(images_dev):
            for group in range(2):
                row = image * 8 + group * LINES
                at = (owner * images_dev + image, pl.ds(group, LINES, stride=2))
                full[at] = spread[row : row + LINES]

    take(me, sent[me])
    fetch.wait()
    lane = iota((1, 128), 1)
    for r in range(rounds):
        ranks = []
        for c in range(2):
            start = pl.multiple_of(me // 2 * 128, 128)
            near = pairs_ref[r, c : c + 1, pl.ds(start, 128)]
            own = jnp.where((lane < 64) == (lax.rem(me, 2) == 0), near, rolled(near, 64, 1))
            rank = jnp.zeros_like(own)
            for k in range(peers):
                rank = rank + (own > ids[r * peers + k, me]).astype(jnp.int32)
            ranks.append(rank)
        products, powers = picks(*ranks, peers)
        chosen[r, :128, :] = products.T.astype(jnp.bfloat16)
        chosen[r, 128:, :] = powers.T.astype(jnp.bfloat16)
    for o in range(1, peers):
        images(o).wait_recv()
        owner = partner(me, o)
        take(owner, held[owner])

    def result(kind, peer):
        step, _ = kinds[kind]
        device = {"date": peer}
        if step:
            device["az"] = az + step
        return pltpu.make_async_remote_copy(
            src_ref=(near_sums.at[kind - 1] if kind else sums).at[peer],
            dst_ref=(near_tiles.at[kind - 1] if kind else tiles).at[me],
            send_sem=send_b.at[kind],
            recv_sem=recv_b.at[kind],
            device_id=device,
            device_id_type=MESH,
        )

    def serve(peer, carry):
        shares = []
        for r in range(rounds):
            real, imag = [], []
            for k in range(peers):
                date = ids[r * peers + k, peer]
                real.append(full[2 * date])
                imag.append(full[2 * date + 1])
            shares.append(shares_of(cell_sums(real, imag)))
        for kind in range(3):
            share = jnp.concatenate([shares[r][kind] for r in range(rounds)], 0)
            if kind:
                near_sums[kind - 1, peer] = share.astype(jnp.bfloat16)
            else:
                sums[peer] = share
        for kind, (step, there) in enumerate(kinds):

            @pl.when(there if step else peer != me)
            def _():
                result(kind, peer).start()

        return carry

    for kind, (step, there) in enumerate(kinds):
        if step:

            @pl.when(jnp.logical_not(there))
            def _():
                near_tiles[2 - kind] = jnp.zeros_like(near_tiles[2 - kind])

    lax.fori_loop(0, peers, serve, 0)
    tiles[me] = sums[me]

    def all_of(src, dst, count, send_sem, recv_sem):
        part = pl.ds(0, count)
        return pltpu.make_async_remote_copy(
            src_ref=src.at[part],
            dst_ref=dst.at[part],
            send_sem=send_sem,
            recv_sem=recv_sem,
            device_id={"date": lax.rem(me + 1, peers)},
            device_id_type=MESH,
        )

    def all_results(kind):
        sems = send_b.at[kind], recv_b.at[kind]
        if kind:
            return all_of(near_sums.at[kind - 1], near_tiles.at[kind - 1], peers, *sems)
        return all_of(sums, tiles, peers - 1, *sems)

    all_results(0).wait_recv()
    for kind, (step, there) in enumerate(kinds):
        if step:

            @pl.when(there)
            def _():
                all_results(3 - kind).wait_recv()

    own, near = [], []
    for j in range(peers):
        own.append(tiles[j])
        sides_sum = near_tiles[0, j].astype(jnp.float32) + near_tiles[1, j].astype(jnp.float32)
        near.append(both_rows(own[-1]) + sides_sum)
    for r in range(rounds):
        at = slice(8 * r, 8 * r + 8)
        table[r] = jnp.concatenate(table_of([x[at] for x in own]), 0)
        boxed_ref[r] = box_of(jnp.concatenate(table_of([x[at] for x in near]), 0))

    all_of(sent, held, peers - 1, send_a, recv_a.at[0]).wait_send()
    all_results(0).wait_send()
    for kind, (step, there) in enumerate(kinds):
        if step:

            @pl.when(there)
            def _():
                all_results(kind).wait_send()


def pairs_kernel(table_ref, boxed_ref, chosen_ref, ifg_hbm, coh_hbm, ifg_ref, coh_ref, sems):
    rounds = table_ref.shape[0]

    def out(r, src, dst, n):
        rows = src.shape[0] // rounds
        at = pl.ds(rows * r, rows)
        return pltpu.make_async_copy(src.at[at], dst.at[at], sems.at[n, r])

    for r in range(rounds):
        means = jnp.dot(
            chosen_ref[r, :128], in_two(table_ref[r]), preferred_element_type=jnp.float32
        )
        for c in range(2):
            for row in range(2):
                part = means[64 * c : 64 * c + 64, 64 * row : 64 * row + 64]
                ifg_ref[pl.ds(256 * r + 2 * c + row, 64, stride=4), :] = part
        out(r, ifg_ref, ifg_hbm, 0).start()
        parts = jnp.dot(
            chosen_ref[r], in_two(boxed_ref[r]), preferred_element_type=jnp.float32
        )
        size = jnp.sqrt(parts[:64] * parts[:64] + parts[64:128] * parts[64:128])
        coherence = size / jnp.sqrt(parts[128:192] * parts[192:])
        for row in range(2):
            part = coherence[:, 64 * row : 64 * row + 64]
            coh_ref[pl.ds(128 * r + row, 64, stride=2), :] = part
        out(r, coh_ref, coh_hbm, 1).start()
    for r in range(rounds):
        out(r, ifg_ref, ifg_hbm, 0).wait()
        out(r, coh_ref, coh_hbm, 1).wait()


def per_device_few(slc, pairs):
    peers = lax.axis_size("date")
    rounds = pairs.shape[0]
    pair_dev = pairs.shape[1] // peers
    date_dev, _, lines, columns = slc.shape
    width = columns // peers
    rows = date_dev * 2 * lines
    cells = columns // SAMPLES
    vmem = pl.BlockSpec(memory_space=pltpu.VMEM)
    hbm = pl.BlockSpec(memory_space=pltpu.HBM)
    dma = pltpu.SemaphoreType.DMA
    found = pl.pallas_call(
        stack_kernel,
        out_shape=(
            jax.ShapeDtypeStruct((rounds, 64, 128), jnp.float32),
            jax.ShapeDtypeStruct((rounds, 64, 128), jnp.float32),
            jax.ShapeDtypeStruct((rounds, 256, 128), jnp.bfloat16),
        ),
        in_specs=[hbm, hbm],
        out_specs=(vmem,) * 3,
        scratch_shapes=[
            pltpu.VMEM(slc.shape, jnp.float32),
            pltpu.VMEM((peers, rows, width), jnp.bfloat16),
            pltpu.VMEM((peers, rows, width), jnp.bfloat16),
            pltpu.VMEM((peers * date_dev * 2, lines, width), jnp.float32),
            pltpu.VMEM((peers, rounds * 8, 128), jnp.float32),
            pltpu.VMEM((peers, rounds * 8, 128), jnp.float32),
            pltpu.VMEM((2, peers, rounds * 8, 128), jnp.bfloat16),
            pltpu.VMEM((2, peers, rounds * 8, 128), jnp.bfloat16),
            pltpu.VMEM((rounds * peers, 128), jnp.int32),
            pltpu.SMEM((rounds * peers, 128), jnp.int32),
            pltpu.VMEM((rounds, 2, pairs.shape[1]), jnp.int32),
            dma,
            dma,
            dma,
            dma((peers,)),
            dma((3,)),
            dma((3,)),
            dma,
        ],
        compiler_params=pltpu.CompilerParams(
            collective_id=0, has_side_effects=True, vmem_limit_bytes=VMEM_LIMIT
        ),
    )(
        pltpu.with_memory_space_constraint(slc, pltpu.HBM),
        pltpu.with_memory_space_constraint(pairs.transpose(0, 2, 1), pltpu.HBM),
    )
    ifg_shape = (rounds * pair_dev * 2 * lines // LINES, cells)
    coh_shape = (rounds * pair_dev * lines // LINES, cells)
    ifg, coh = pl.pallas_call(
        pairs_kernel,
        out_shape=(
            jax.ShapeDtypeStruct(ifg_shape, jnp.float32),
            jax.ShapeDtypeStruct(coh_shape, jnp.float32),
        ),
        in_specs=[vmem] * 3,
        out_specs=(hbm, hbm),
        scratch_shapes=[
            pltpu.VMEM(ifg_shape, jnp.float32),
            pltpu.VMEM(coh_shape, jnp.float32),
            dma((2, rounds)),
        ],
        compiler_params=pltpu.CompilerParams(vmem_limit_bytes=VMEM_LIMIT),
    )(*found)
    return (
        ifg.reshape(rounds, pair_dev, 2, lines // LINES, cells),
        coh.reshape(rounds, pair_dev, lines // LINES, cells),
    )


def per_device(slc, pairs):
    peers = lax.axis_size("date")
    lines, columns = slc.shape[2:]
    pair_dev = pairs.shape[1] // peers
    few = (peers, pair_dev, lines, columns) == (8, 64, 2 * LINES, 64 * SAMPLES)
    return per_device_few(slc, pairs) if few else per_device_general(slc, pairs)


def solution(mesh):
    return jax.shard_map(
        per_device,
        mesh=mesh,
        in_specs=(P("date", None, "az", None), P()),
        out_specs=(P(None, "date", None, "az", None), P(None, "date", "az", None)),
        check_vma=False,
    )
```

```python
import jax
import jax.numpy as jnp
from jax import lax
from jax.experimental import pallas as pl
from jax.experimental.pallas import tpu as pltpu
from jax.sharding import PartitionSpec as P

CAP = 2
FAR_FIRST = (7, 5, 6, 3, 4, 2, 1)
VMEM_LIMIT = 4 << 20


def with_halo(shard, sides, width):
    for axis, dim in sides:
        peers, length = (lax.axis_size(axis), shard.shape[dim])
        up = [(i, (i + 1) % peers) for i in range(peers - 1)]
        down = [(j, i) for i, j in up]
        last = lax.slice_in_dim(shard, length - width, length, axis=dim)
        first = lax.slice_in_dim(shard, 0, width, axis=dim)
        before = lax.ppermute(last, axis, up)
        after = lax.ppermute(first, axis, down)
        shard = jnp.concatenate([before, shard, after], axis=dim)
    return shard


def multilook(field):
    shape = field.shape
    blocks = field.reshape(shape[:-2] + (shape[-2] // 4, 4, shape[-1] // 16, 16))
    return blocks.mean(axis=(-3, -1))


def pair_looks(tiles):
    first = tiles[:, 0].astype(jnp.float32)
    second = tiles[:, 1].astype(jnp.float32)
    first_re, first_im = (first[:, 0], first[:, 1])
    second_re, second_im = (second[:, 0], second[:, 1])
    prod_re = first_re * second_re + first_im * second_im
    prod_im = first_im * second_re - first_re * second_im
    power_a = first_re * first_re + first_im * first_im
    power_b = second_re * second_re + second_im * second_im
    return jnp.stack(
        [multilook(prod_re), multilook(prod_im), multilook(power_a), multilook(power_b)], axis=1
    )


def coherence_from(padded):
    lines = padded.shape[-2] - 4
    columns = padded.shape[-1]
    az_sum = padded[..., 0:lines, :]
    for offset in range(1, 5):
        az_sum = az_sum + padded[..., offset : offset + lines, :]
    widths = [(0, 0)] * (az_sum.ndim - 1) + [(2, 2)]
    wide = jnp.pad(az_sum, widths)
    boxed = wide[..., 0:columns]
    for offset in range(1, 5):
        boxed = boxed + wide[..., offset : offset + columns]
    numer = jnp.sqrt(boxed[..., 0, :, :] ** 2 + boxed[..., 1, :, :] ** 2)
    return numer / jnp.sqrt(boxed[..., 2, :, :] * boxed[..., 3, :, :])


def per_device_general(slc, pairs):
    date_count = lax.axis_size("date")
    own_index = lax.axis_index("date")
    date_dev = slc.shape[0]
    pair_dev = pairs.shape[1] // date_count
    tile_shape = slc.shape[1:]
    quantized = lax.optimization_barrier(slc.astype(jnp.bfloat16))
    all_ids = jnp.arange(date_count * date_dev, dtype=jnp.int32)
    local_ids = own_index * date_dev + jnp.arange(date_dev, dtype=jnp.int32)
    local_pos = jnp.arange(date_dev, dtype=jnp.int32)
    slot_ids = jnp.arange(CAP, dtype=jnp.int32)
    looks_list = []
    for round_index in range(pairs.shape[0]):
        block = pairs[round_index]
        own_pairs = lax.dynamic_slice_in_dim(block, own_index * pair_dev, pair_dev, 0)
        entries = own_pairs.reshape(-1)
        wanted = block.reshape(date_count, 2 * pair_dev)
        needed = jnp.any(wanted[:, :, None] == local_ids[None, None, :], axis=1).astype(jnp.int32)
        ranks = jnp.cumsum(needed, axis=1) - needed
        picked = needed[:, None, :] * (ranks[:, None, :] == slot_ids[None, :, None]).astype(
            jnp.int32
        )
        source_local = jnp.sum(picked * local_pos[None, None, :], axis=2)
        present = jnp.sum(picked, axis=2) > 0
        outgoing = jnp.take(quantized, source_local.reshape(-1), axis=0).reshape(
            (date_count, CAP) + tile_shape
        )
        outgoing = jnp.where(present[:, :, None, None, None], outgoing, jnp.zeros((), jnp.bfloat16))
        incoming = lax.all_to_all(outgoing, "date", split_axis=0, concat_axis=0, tiled=True)
        matches = entries[:, None] == all_ids[None, :]
        my_need = jnp.any(matches, axis=0).astype(jnp.int32).reshape(date_count, date_dev)
        my_rank = (jnp.cumsum(my_need, axis=1) - my_need).reshape(-1)
        entry_slot = jnp.sum(jnp.where(matches, my_rank[None, :], 0), axis=1)
        position = entries // date_dev * CAP + entry_slot
        fetched = jnp.take(incoming.reshape((date_count * CAP,) + tile_shape), position, axis=0)
        looks = pair_looks(fetched.reshape((pair_dev, 2) + tile_shape))
        looks_list.append(looks)
    stacked = jnp.stack(looks_list, axis=0)
    padded = with_halo(stacked, (("az", 3),), 2)
    coherence = coherence_from(padded)
    interferogram = stacked[:, :, 0:2]
    return (interferogram, coherence)


LINES, SAMPLES = 4, 16
STEPS = ((1, 8, 1), (1, 8, 2), (1, 8, 4), (1, 8, 8), (0, 2, 1), (0, 2, 2))


def iota(shape, dim):
    return lax.broadcasted_iota(jnp.int32, shape, dim)


def place_of(leaf):
    bit = [(leaf >> n) & 1 for n in range(6)]
    return 32 * bit[2] + 16 * bit[1] + 8 * bit[0] + 4 * bit[5] + 2 * bit[4] + bit[3]


def rolled(x, shift, dim):
    return pltpu.roll(x, shift % x.shape[dim], dim)


def lower(shape, dim, far):
    return (iota(shape, dim) & far) == 0


def join(one, two, dim, far):
    low = lower(one.shape, dim, far)
    kept = jnp.where(low, one, two)
    other = jnp.where(low, two, one)
    return kept + rolled(other, -far, dim)


def cell_sums(real, imag):
    count = len(real)
    couples = [(i, j) for i in range(count) for j in range(i + 1, count)]
    dim, unit, dist = STEPS[0]
    low = lower(real[0].shape, dim, unit * dist)
    mixed = []
    for re, im in zip(real, imag):
        kept = (jnp.where(low, re, im), jnp.where(low, im, -re))
        other = (jnp.where(low, im, re), jnp.where(low, -re, im))
        mixed.append((kept, other))

    def power(i):
        return real[i] * real[i] + imag[i] * imag[i]

    def first(place):
        n = (place & 7) + (place >> 4 << 3)
        if n >= len(couples):
            i = n - len(couples)
            return join(power(i), power(i + count // 2), dim, unit * dist)
        i, j = couples[n]
        kept, other = [a * real[j] + b * imag[j] for a, b in mixed[i]]
        return kept + rolled(other, -unit * dist, dim)

    def build(level, base):
        if level == 1:
            return first(place_of(base))
        dim, unit, dist = STEPS[level - 1]
        one = build(level - 1, base)
        two = build(level - 1, base + (1 << (level - 1)))
        return join(one, two, dim, unit * dist)

    return build(len(STEPS), 0)


def in_two(x):
    high = x.astype(jnp.bfloat16)
    low = (x - high.astype(jnp.float32)).astype(jnp.bfloat16)
    return jnp.concatenate([high, low], 0)


def sample_order():
    src, dst = iota((128, 128), 0), iota((128, 128), 1)
    hit = dst == (src % SAMPLES) * (128 // SAMPLES) + src // SAMPLES
    return jnp.where(hit, 1.0 / 8, 0.0).astype(jnp.bfloat16)


def table_of(tiles):
    lane, sub = iota((8, 128), 1), iota((8, 128), 0)
    tiles = list(tiles)
    for b in range(3):
        dist = 8 << b
        low = (lane & dist) == 0
        for j in range(8):
            if not j >> b & 1:
                one, two = tiles[j], tiles[j | 1 << b]
                tiles[j] = jnp.where(low, one, rolled(two, dist, 1))
                tiles[j | 1 << b] = jnp.where(low, rolled(one, -dist, 1), two)
    even, first = (sub & 1) == 0, lane < 64
    out = []
    for tile in tiles:
        far = rolled(tile, 64, 1)
        moved = jnp.where(even, rolled(far, -1, 0), rolled(far, 1, 0))
        out.append(jnp.where(even == first, tile, moved))
    return out


def both_rows(x):
    odd = (iota(x.shape, 0) & 1) == 1
    return x + jnp.where(odd, rolled(x, 1, 0), rolled(x, -1, 0))


def shares_of(x):
    odd = (iota(x.shape, 0) & 1) == 1
    both = both_rows(x)
    return x, jnp.where(odd, both, x), jnp.where(odd, x, both)


def box_of(both):
    cell = iota(both.shape, 1) & 63
    out = both
    for o in (-2, -1, 1, 2):
        valid = (cell + o >= 0) & (cell + o < 64)
        out = out + jnp.where(valid, rolled(both, -o, 1), 0.0)
    return out


def pick(places, values):
    return jnp.where(iota((128, 128), 0) & 63 == places, values, 0.0)


def spot(n):
    return (n & 7) + (n >> 3 << 4)


def picks(rank_a, rank_b, count):
    first = iota(rank_a.shape, 1) < 64
    low, high = jnp.minimum(rank_a, rank_b), jnp.maximum(rank_a, rank_b)
    place = ((low * (2 * count - 1 - low)) >> 1) + high - low - 1
    sign = jnp.where(first | (rank_a < rank_b), 1.0, -1.0)
    products = pick(spot(place) + jnp.where(first, 0, 8), sign)
    rank = jnp.where(first, rank_a, rank_b)
    half = count // 2
    place = spot(count * (count - 1) // 2 + (rank & (half - 1)))
    powers = pick(place + jnp.where(rank < half, 0, 8), jnp.ones_like(sign))
    return products, powers


MESH = pl.DeviceIdType.MESH


def partner(me, m):
    out = 0
    for n in range(3):
        mine, other = me // 2**n % 2, m // 2**n % 2
        out = out + 2**n * (mine + other - 2 * mine * other)
    return out


def list_dates(pairs, dates, peers):
    length = pairs.shape[1]
    part = length // peers
    date = iota((dates, length), 0)
    named = (pairs[0:1] == date) | (pairs[1:2] == date)
    parts = iota((length, 128), 0) // part == iota((length, 128), 1)
    dims = (((1,), (0,)), ((), ()))
    one = jnp.bfloat16
    counts = lax.dot_general(
        named.astype(jnp.float32).astype(one),
        parts.astype(jnp.float32).astype(one),
        dims,
        preferred_element_type=jnp.float32,
    )
    needed = counts > 0.5
    before = iota((dates, dates), 1) < iota((dates, dates), 0)
    rank = lax.dot_general(
        before.astype(jnp.float32).astype(one),
        needed.astype(jnp.float32).astype(one),
        dims,
        preferred_element_type=jnp.float32,
    )
    rank = jnp.where(needed, rank, -1.0).astype(jnp.int32)
    date = iota(rank.shape, 0)
    rows = [jnp.sum(jnp.where(rank == k, date, 0), axis=0, keepdims=True) for k in range(peers)]
    return jnp.concatenate(rows, 0)


def stack_kernel(
    slc_ref,
    pairs_hbm,
    table,
    boxed_ref,
    chosen,
    lines,
    sent,
    held,
    full,
    sums,
    tiles,
    near_sums,
    near_tiles,
    listed,
    ids,
    pairs_ref,
    pairs_sem,
    line_sem,
    send_a,
    recv_a,
    send_b,
    recv_b,
    list_sem,
):
    peers, az_size = lax.axis_size("date"), lax.axis_size("az")
    me, az = lax.axis_index("date"), lax.axis_index("az")
    date_dev = slc_ref.shape[0]
    rounds = pairs_ref.shape[0]
    width = slc_ref.shape[3] // peers
    images_dev = 2 * date_dev
    sides = ((-1, az > 0), (1, az < az_size - 1))
    kinds = ((0, None),) + sides

    named = pltpu.make_async_copy(pairs_hbm, pairs_ref, pairs_sem)
    barrier = pltpu.get_barrier_semaphore()
    for n in range(date_dev):
        pltpu.make_async_copy(slc_ref.at[n], lines.at[n], line_sem).start()
    named.start()
    for o in range(1, peers):
        pl.semaphore_signal(
            barrier, inc=1, device_id={"date": lax.rem(me + o, peers)}, device_id_type=MESH
        )
    for step, there in sides:

        @pl.when(there)
        def _():
            pl.semaphore_signal(barrier, inc=1, device_id={"az": az + step}, device_id_type=MESH)

    rows_date = sent.shape[1] // date_dev
    pltpu.make_async_copy(slc_ref, lines, line_sem).wait()
    for n in range(date_dev):
        for j in range(peers):
            part = lines[n, :, :, j * width : (j + 1) * width]
            at = slice(n * rows_date, (n + 1) * rows_date)
            sent[j, at] = part.reshape(rows_date, width).astype(jnp.bfloat16)
    greeted = peers - 1 + (az > 0).astype(jnp.int32) + (az < az_size - 1).astype(jnp.int32)
    pl.semaphore_wait(barrier, greeted)

    def images(o):
        peer = partner(me, o)
        return pltpu.make_async_remote_copy(
            src_ref=sent.at[peer],
            dst_ref=held.at[me],
            send_sem=send_a,
            recv_sem=recv_a.at[o],
            device_id={"date": peer},
            device_id_type=MESH,
        )

    for o in FAR_FIRST:
        images(o).start()
    named.wait()
    for r in range(rounds):
        listed[r * peers : (r + 1) * peers, :] = list_dates(
            pairs_ref[r], date_dev * peers, peers
        )
    fetch = pltpu.make_async_copy(listed, ids, list_sem)
    fetch.start()
    order = sample_order()

    def take(owner, block):
        spread = jnp.dot(block, order, preferred_element_type=jnp.float32)
        for image in range(images_dev):
            for group in range(2):
                row = image * 8 + group * LINES
                at = (owner * images_dev + image, pl.ds(group, LINES, stride=2))
                full[at] = spread[row : row + LINES]

    take(me, sent[me])
    fetch.wait()
    lane = iota((1, 128), 1)
    for r in range(rounds):
        ranks = []
        for c in range(2):
            start = pl.multiple_of(me // 2 * 128, 128)
            near = pairs_ref[r, c : c + 1, pl.ds(start, 128)]
            own = jnp.where((lane < 64) == (lax.rem(me, 2) == 0), near, rolled(near, 64, 1))
            rank = jnp.zeros_like(own)
            for k in range(peers):
                rank = rank + (own > ids[r * peers + k, me]).astype(jnp.int32)
            ranks.append(rank)
        products, powers = picks(*ranks, peers)
        chosen[r, :128, :] = products.T.astype(jnp.bfloat16)
        chosen[r, 128:, :] = powers.T.astype(jnp.bfloat16)
    for o in range(1, peers):
        images(o).wait_recv()
        owner = partner(me, o)
        take(owner, held[owner])

    def result(kind, peer):
        step, _ = kinds[kind]
        device = {"date": peer}
        if step:
            device["az"] = az + step
        return pltpu.make_async_remote_copy(
            src_ref=(near_sums.at[kind - 1] if kind else sums).at[peer],
            dst_ref=(near_tiles.at[kind - 1] if kind else tiles).at[me],
            send_sem=send_b.at[kind],
            recv_sem=recv_b.at[kind],
            device_id=device,
            device_id_type=MESH,
        )

    def serve(peer, carry):
        shares = []
        for r in range(rounds):
            real, imag = [], []
            for k in range(peers):
                date = ids[r * peers + k, peer]
                real.append(full[2 * date])
                imag.append(full[2 * date + 1])
            shares.append(shares_of(cell_sums(real, imag)))
        for kind in range(3):
            share = jnp.concatenate([shares[r][kind] for r in range(rounds)], 0)
            if kind:
                near_sums[kind - 1, peer] = share.astype(jnp.bfloat16)
            else:
                sums[peer] = share
        for kind, (step, there) in enumerate(kinds):

            @pl.when(there if step else peer != me)
            def _():
                result(kind, peer).start()

        return carry

    for kind, (step, there) in enumerate(kinds):
        if step:

            @pl.when(jnp.logical_not(there))
            def _():
                near_tiles[2 - kind] = jnp.zeros_like(near_tiles[2 - kind])

    lax.fori_loop(0, peers, serve, 0)
    tiles[me] = sums[me]

    def all_of(src, dst, count, send_sem, recv_sem):
        part = pl.ds(0, count)
        return pltpu.make_async_remote_copy(
            src_ref=src.at[part],
            dst_ref=dst.at[part],
            send_sem=send_sem,
            recv_sem=recv_sem,
            device_id={"date": lax.rem(me + 1, peers)},
            device_id_type=MESH,
        )

    def all_results(kind):
        sems = send_b.at[kind], recv_b.at[kind]
        if kind:
            return all_of(near_sums.at[kind - 1], near_tiles.at[kind - 1], peers, *sems)
        return all_of(sums, tiles, peers - 1, *sems)

    all_results(0).wait_recv()
    for kind, (step, there) in enumerate(kinds):
        if step:

            @pl.when(there)
            def _():
                all_results(3 - kind).wait_recv()

    own, near = [], []
    for j in range(peers):
        own.append(tiles[j])
        sides_sum = near_tiles[0, j].astype(jnp.float32) + near_tiles[1, j].astype(jnp.float32)
        near.append(both_rows(own[-1]) + sides_sum)
    for r in range(rounds):
        at = slice(8 * r, 8 * r + 8)
        table[r] = jnp.concatenate(table_of([x[at] for x in own]), 0)
        boxed_ref[r] = box_of(jnp.concatenate(table_of([x[at] for x in near]), 0))

    all_of(sent, held, peers - 1, send_a, recv_a.at[0]).wait_send()
    all_results(0).wait_send()
    for kind, (step, there) in enumerate(kinds):
        if step:

            @pl.when(there)
            def _():
                all_results(kind).wait_send()


def pairs_kernel(table_ref, boxed_ref, chosen_ref, ifg_hbm, coh_hbm, ifg_ref, coh_ref, sems):
    rounds = table_ref.shape[0]

    def out(r, src, dst, n):
        rows = src.shape[0] // rounds
        at = pl.ds(rows * r, rows)
        return pltpu.make_async_copy(src.at[at], dst.at[at], sems.at[n, r])

    for r in range(rounds):
        means = jnp.dot(
            chosen_ref[r, :128], in_two(table_ref[r]), preferred_element_type=jnp.float32
        )
        for c in range(2):
            for row in range(2):
                part = means[64 * c : 64 * c + 64, 64 * row : 64 * row + 64]
                ifg_ref[pl.ds(256 * r + 2 * c + row, 64, stride=4), :] = part
        out(r, ifg_ref, ifg_hbm, 0).start()
        parts = jnp.dot(
            chosen_ref[r], in_two(boxed_ref[r]), preferred_element_type=jnp.float32
        )
        size = jnp.sqrt(parts[:64] * parts[:64] + parts[64:128] * parts[64:128])
        coherence = size / jnp.sqrt(parts[128:192] * parts[192:])
        for row in range(2):
            part = coherence[:, 64 * row : 64 * row + 64]
            coh_ref[pl.ds(128 * r + row, 64, stride=2), :] = part
        out(r, coh_ref, coh_hbm, 1).start()
    for r in range(rounds):
        out(r, ifg_ref, ifg_hbm, 0).wait()
        out(r, coh_ref, coh_hbm, 1).wait()


def per_device_few(slc, pairs):
    peers = lax.axis_size("date")
    rounds = pairs.shape[0]
    pair_dev = pairs.shape[1] // peers
    date_dev, _, lines, columns = slc.shape
    width = columns // peers
    rows = date_dev * 2 * lines
    cells = columns // SAMPLES
    vmem = pl.BlockSpec(memory_space=pltpu.VMEM)
    hbm = pl.BlockSpec(memory_space=pltpu.HBM)
    dma = pltpu.SemaphoreType.DMA
    found = pl.pallas_call(
        stack_kernel,
        out_shape=(
            jax.ShapeDtypeStruct((rounds, 64, 128), jnp.float32),
            jax.ShapeDtypeStruct((rounds, 64, 128), jnp.float32),
            jax.ShapeDtypeStruct((rounds, 256, 128), jnp.bfloat16),
        ),
        in_specs=[hbm, hbm],
        out_specs=(vmem,) * 3,
        scratch_shapes=[
            pltpu.VMEM(slc.shape, jnp.float32),
            pltpu.VMEM((peers, rows, width), jnp.bfloat16),
            pltpu.VMEM((peers, rows, width), jnp.bfloat16),
            pltpu.VMEM((peers * date_dev * 2, lines, width), jnp.float32),
            pltpu.VMEM((peers, rounds * 8, 128), jnp.float32),
            pltpu.VMEM((peers, rounds * 8, 128), jnp.float32),
            pltpu.VMEM((2, peers, rounds * 8, 128), jnp.bfloat16),
            pltpu.VMEM((2, peers, rounds * 8, 128), jnp.bfloat16),
            pltpu.VMEM((rounds * peers, 128), jnp.int32),
            pltpu.SMEM((rounds * peers, 128), jnp.int32),
            pltpu.VMEM((rounds, 2, pairs.shape[1]), jnp.int32),
            dma,
            dma,
            dma,
            dma((peers,)),
            dma((3,)),
            dma((3,)),
            dma,
        ],
        compiler_params=pltpu.CompilerParams(
            collective_id=0, has_side_effects=True, vmem_limit_bytes=VMEM_LIMIT
        ),
    )(
        pltpu.with_memory_space_constraint(slc, pltpu.HBM),
        pltpu.with_memory_space_constraint(pairs.transpose(0, 2, 1), pltpu.HBM),
    )
    ifg_shape = (rounds * pair_dev * 2 * lines // LINES, cells)
    coh_shape = (rounds * pair_dev * lines // LINES, cells)
    ifg, coh = pl.pallas_call(
        pairs_kernel,
        out_shape=(
            jax.ShapeDtypeStruct(ifg_shape, jnp.float32),
            jax.ShapeDtypeStruct(coh_shape, jnp.float32),
        ),
        in_specs=[vmem] * 3,
        out_specs=(hbm, hbm),
        scratch_shapes=[
            pltpu.VMEM(ifg_shape, jnp.float32),
            pltpu.VMEM(coh_shape, jnp.float32),
            dma((2, rounds)),
        ],
        compiler_params=pltpu.CompilerParams(vmem_limit_bytes=VMEM_LIMIT),
    )(*found)
    return (
        ifg.reshape(rounds, pair_dev, 2, lines // LINES, cells),
        coh.reshape(rounds, pair_dev, lines // LINES, cells),
    )


def per_device(slc, pairs):
    peers = lax.axis_size("date")
    lines, columns = slc.shape[2:]
    pair_dev = pairs.shape[1] // peers
    few = (peers, pair_dev, lines, columns) == (8, 64, 2 * LINES, 64 * SAMPLES)
    return per_device_few(slc, pairs) if few else per_device_general(slc, pairs)


def solution(mesh):
    return jax.shard_map(
        per_device,
        mesh=mesh,
        in_specs=(P("date", None, "az", None), P()),
        out_specs=(P(None, "date", None, "az", None), P(None, "date", "az", None)),
        check_vma=False,
    )
```
